32 devices in a mesh: dp: 8 (over z, core), tensor: 4 (over y, x).
Axes of the slice: x: 2, y: 2, z: 4, core: 2. Of those that a mesh axis runs over, the one named last changes fastest.
Arguments:
- inputs: bfloat16 [8, 1024, 1024], P('dp'), may hold values from -6 to 6
- cotangent: bfloat16 [8, 1024, 1024], P('dp'), may hold values from -6 to 6
- groups: int32 [8], P('dp'), may hold values from 0 to 7
- counts: int32 [8], replicated, may hold values from 128 to 512
- vector_parameters: float32 [6, 1024], replicated, may hold values from -0.9 to 1.4, as said below
- query_value_bias: float32 [2, 1024], P(None, 'tensor'), may hold values from -1.8 to 1.8
- hidden_bias: float32 [4096], P('tensor'), may hold values from -1.8 to 1.8
- query_key_value_weight: bfloat16 [3, 1024, 1024], P(None, None, 'tensor'), may hold values from -0.1875 to 0.1875
- attention_output_weight: bfloat16 [1024, 1024], P('tensor'), may hold values from -0.75 to 0.75
- hidden_weight: bfloat16 [1024, 4096], P(None, 'tensor'), may hold values from -0.1875 to 0.1875
- hidden_output_weight: bfloat16 [4096, 1024], P('tensor'), may hold values from -0.09375 to 0.09375
- adapter_down: float32 [2, 1024, 4], replicated, may hold values from -0.1875 to 0.1875
- adapter_up: float32 [2, 4, 1024], replicated, may hold values from -0.18 to 0.18
- momentum_down: float32 [2, 1024, 4], replicated, may hold values from -0.039774757 to 0.039774757
- momentum_up: float32 [2, 4, 1024], replicated, may hold values from -0.079549514 to 0.079549514
- average_down: float32 [2, 1024, 4], replicated, may hold values from -0.1875 to 0.1875
- average_up: float32 [2, 4, 1024], replicated, may hold values from -0.18 to 0.18
Outputs:
- block_out: bfloat16 [8, 1024, 1024], P('dp')
- input_grad: bfloat16 [8, 1024, 1024], P('dp')
- down_gradient: float32 [2, 1024, 4], replicated
- up_gradient: float32 [2, 4, 1024], replicated
- updated_momentum_down: float32 [2, 1024, 4], replicated
- updated_momentum_up: float32 [2, 4, 1024], replicated
- updated_down: float32 [2, 1024, 4], replicated
- updated_up: float32 [2, 4, 1024], replicated
- updated_average_down: float32 [2, 1024, 4], replicated
- updated_average_up: float32 [2, 4, 1024], replicated
- copy_a: bfloat16 [2, 1024, 4], replicated
- copy_b: bfloat16 [2, 4, 1024], replicated
The draws below stay inside these ranges and needn't reach their ends.
Inputs may be any that keep to these rules, and one draw needn't show every extreme that they name: `vector_parameters`: rows 0 and 2 are gains, the other rows shifts and biases.
All inputs are finite; a program needn't handle non-finite values.
Results may differ from the reference program's by a relative error of at most 0.018.
Values may be sent and summed in bfloat16 or wider, within the bound.
No kernel may reach another device: no remote copies, remote signals or barrier semaphores. Data moves between devices by JAX's collectives and lax.ppermute only.
A program may use at most 128 MiB of HBM per device.

```python
import math
import jax
import jax.numpy as jnp
from jax import lax

MODEL_WIDTH = 1024
HEADS = 16
HEAD = 64
FF = 4096
ADAPTER_RANK = 4
GROUPS = 8
LENGTH = 1024
SEQS = 8
TOKENS = 8192
N_TENSOR = 4


def draw_vector_parameters(key, part):
    first_key, second_key = jax.random.split(key)
    gains = jax.random.uniform(first_key, (2, MODEL_WIDTH), jnp.float32, 0.6, 1.4)
    shifts = 0.3 * jax.random.truncated_normal(second_key, -3.0, 3.0, (4, MODEL_WIDTH), jnp.float32)
    return jnp.stack([gains[0], shifts[0], gains[1], shifts[1], shifts[2], shifts[3]]).astype(jnp.float32)


def plant(entries, rng, low, high):
    longest = entries.shape.index(max(entries.shape))
    spots = []
    for shift in (0, 1):
        where = [jax.random.randint(jax.random.fold_in(rng, axis), (), 0, length) for axis, length in enumerate(entries.shape)]
        where[longest] = (where[longest] + shift) % entries.shape[longest]
        spots.append(tuple(where))
    return entries.at[spots[0]].set(low).at[spots[1]].set(high)


def shard_levels(stream_key, shape, pieces, smallest, high):
    def one(dim, shards_of):
        steps = jax.random.uniform(jax.random.fold_in(jax.random.fold_in(stream_key, 6), dim), (shards_of,), jnp.float32, smallest / len(pieces), high / len(pieces))
        return jnp.repeat(jnp.exp(steps), shape[dim] // shards_of).reshape((-1,) + (1,) * (len(shape) - dim - 1))

    loudness = one(*pieces[0])
    for cut in pieces[1:]:
        loudness = loudness * one(*cut)
    return loudness


def normal_values(own_key, extent, scale, limit, pieces=(), held_as=jnp.bfloat16):
    level = shard_levels(own_key, extent, pieces, -0.22, 0.18) if pieces else 1.0
    values = jax.random.normal(own_key, extent, jnp.float32) * scale * level
    return jnp.minimum(jnp.maximum(values, -limit), limit).astype(held_as)


def setup_inputs(seed: int = 0) -> dict:
    key_of = jax.random.split(jax.random.key(seed), 18)
    inputs = normal_values(key_of[0], (SEQS, LENGTH, MODEL_WIDTH), 1.0, 6.0, ((0, 8),))
    cotangent = normal_values(key_of[1], (SEQS, LENGTH, MODEL_WIDTH), 1.0, 6.0, ((0, 8),))
    groups = plant(jax.random.randint(key_of[2], (SEQS,), 0, GROUPS), jax.random.fold_in(key_of[2], 1), 0, GROUPS - 1).astype(jnp.int32)
    counts = plant(jax.random.randint(key_of[3], (GROUPS,), 128, 513), jax.random.fold_in(key_of[3], 1), 128, 512).astype(jnp.int32)
    vector_parameters = draw_vector_parameters(jax.random.fold_in(key_of[17], 71), 0)
    query_value_bias = normal_values(key_of[5], (2, MODEL_WIDTH), 0.3, 1.8, ((1, 4),), jnp.float32)
    hidden_bias = normal_values(key_of[6], (FF,), 0.3, 1.8, ((0, 4),), jnp.float32)
    query_key_value_weight = normal_values(key_of[7], (3, MODEL_WIDTH, MODEL_WIDTH), MODEL_WIDTH ** -0.5, 0.1875, ((2, 4),))
    attention_output_weight = normal_values(key_of[8], (MODEL_WIDTH, MODEL_WIDTH), (MODEL_WIDTH // 16) ** -0.5, 0.75, ((0, 4),))
    hidden_weight = normal_values(key_of[9], (MODEL_WIDTH, FF), MODEL_WIDTH ** -0.5, 0.1875, ((1, 4),))
    hidden_output_weight = normal_values(key_of[10], (FF, MODEL_WIDTH), FF ** -0.5, 0.09375, ((0, 4),))
    adapter_down = normal_values(key_of[11], (2, MODEL_WIDTH, ADAPTER_RANK), MODEL_WIDTH ** -0.5, 0.1875, (), jnp.float32)
    adapter_up = normal_values(key_of[12], (2, ADAPTER_RANK, MODEL_WIDTH), 0.03, 0.18, (), jnp.float32)
    momentum_down = normal_values(key_of[13], (2, MODEL_WIDTH, ADAPTER_RANK), (0.6 / TOKENS ** 0.5), 0.039774757, (), jnp.float32)
    momentum_up = normal_values(key_of[14], (2, ADAPTER_RANK, MODEL_WIDTH), (1.2 / TOKENS ** 0.5), 0.079549514, (), jnp.float32)
    average_down = normal_values(key_of[15], (2, MODEL_WIDTH, ADAPTER_RANK), MODEL_WIDTH ** -0.5, 0.1875, (), jnp.float32)
    average_up = normal_values(key_of[16], (2, ADAPTER_RANK, MODEL_WIDTH), 0.03, 0.18, (), jnp.float32)
    return dict(inputs=inputs, cotangent=cotangent, groups=groups, counts=counts, vector_parameters=vector_parameters, query_value_bias=query_value_bias, hidden_bias=hidden_bias, query_key_value_weight=query_key_value_weight, attention_output_weight=attention_output_weight, hidden_weight=hidden_weight, hidden_output_weight=hidden_output_weight, adapter_down=adapter_down, adapter_up=adapter_up, momentum_down=momentum_down, momentum_up=momentum_up, average_down=average_down, average_up=average_up)


@jax.custom_vjp
def reduced_rows(v):
    return lax.optimization_barrier(v.astype(jnp.bfloat16)).astype(jnp.float32)

@jax.custom_vjp
def reduced_backward(v):
    return v

def low_keep(v):
    return (reduced_rows(v), None)

def low_pass(kept, grad):
    return (grad,)

def back_keep(v):
    return (v, None)

def back_low(kept, grad):
    return (reduced_rows(grad),)
reduced_rows.defvjp(low_keep, low_pass)
reduced_backward.defvjp(back_keep, back_low)
NORM_EPS = 1e-05
ADAPTER_SCALE = 8.0
MASK_FILL = -1e+30
MOMENTUM_FACTOR = 0.9
AVERAGE_KEEP = 0.8
RATE_BASE = 0.025
WEIGHT_DECAY = 0.005
COUNT_BASE = 256.0

def layer_norm(value_rows, norm_gain, norm_bias):
    center = value_rows - lax.optimization_barrier(jnp.mean(value_rows, axis=-1, keepdims=True))
    spread = lax.optimization_barrier(jnp.mean(center * center, axis=-1, keepdims=True))
    return center * lax.rsqrt(spread + NORM_EPS) * norm_gain + norm_bias

def update_step(gradient_term, moment, weight_matrix, average, learning_rate):
    updated_moment = MOMENTUM_FACTOR * moment + gradient_term
    updated_weight = weight_matrix * (1.0 - learning_rate * WEIGHT_DECAY * ADAPTER_SCALE) - learning_rate * (gradient_term + MOMENTUM_FACTOR * updated_moment)
    new_average = AVERAGE_KEEP * average + (1.0 - AVERAGE_KEEP) * updated_weight
    return (updated_moment, updated_weight, new_average)

def reference(inputs, cotangent, groups, counts, vector_parameters, query_value_bias, hidden_bias, query_key_value_weight, attention_output_weight, hidden_weight, hidden_output_weight, adapter_down, adapter_up, momentum_down, momentum_up, average_down, average_up):
    highest_precision = lax.Precision.HIGHEST
    qkv_full = query_key_value_weight.astype(jnp.float32)
    out_blocks = attention_output_weight.astype(jnp.float32).reshape(N_TENSOR, MODEL_WIDTH // N_TENSOR, MODEL_WIDTH)
    fc_full = hidden_weight.astype(jnp.float32)
    proj_blocks = hidden_output_weight.astype(jnp.float32).reshape(N_TENSOR, FF // N_TENSOR, MODEL_WIDTH)
    positions = jnp.arange(LENGTH)
    causal = positions[:, None] >= positions[None, :]
    scale_att = HEAD ** (-0.5)

    def split_heads(matrix):
        return matrix.reshape(LENGTH, HEADS, HEAD).transpose(1, 0, 2)

    def layer_block(sequence_input, down_matrix, up_matrix):
        first_norm_output = reduced_rows(layer_norm(sequence_input, vector_parameters[0], vector_parameters[1]))
        projected_rows = jnp.einsum('rd,cde->cre', first_norm_output, qkv_full, precision=highest_precision)
        adapter_input = reduced_rows(jnp.einsum('wo,qob->qwb', first_norm_output, reduced_rows(down_matrix), precision=highest_precision))
        adapter_output = jnp.einsum('iga,iaj->igj', adapter_input, reduced_rows(up_matrix), precision=highest_precision)
        query_rows = reduced_rows(reduced_backward(projected_rows[0] + query_value_bias[0] + ADAPTER_SCALE * adapter_output[0]))
        keys = reduced_rows(reduced_backward(projected_rows[1]))
        value_rows = reduced_rows(reduced_backward(projected_rows[2] + query_value_bias[1] + ADAPTER_SCALE * adapter_output[1]))
        raw_scores = jnp.einsum('hqe,hke->hqk', split_heads(query_rows), split_heads(keys), precision=highest_precision) * scale_att
        scores = jnp.where(causal[None], reduced_backward(raw_scores), MASK_FILL)
        probs = reduced_rows(jax.nn.softmax(scores, axis=-1))
        heads_out = reduced_rows(reduced_backward(jnp.einsum('hqk,hke->hqe', probs, split_heads(value_rows), precision=highest_precision)))
        merged = heads_out.transpose(1, 0, 2).reshape(LENGTH, N_TENSOR, MODEL_WIDTH // N_TENSOR)
        attn_terms = jnp.einsum('lgc,gcd->gld', merged, out_blocks, precision=highest_precision)
        resid = sequence_input + reduced_backward(lax.optimization_barrier(jnp.sum(reduced_rows(attn_terms), axis=0))) + vector_parameters[4]
        norm2 = reduced_rows(layer_norm(resid, vector_parameters[2], vector_parameters[3]))
        preact = reduced_backward(jnp.dot(norm2, fc_full, precision=highest_precision) + hidden_bias)
        act_low = reduced_rows(jax.nn.gelu(preact, approximate=True))
        mlp_terms = jnp.einsum('lgc,gcd->gld', act_low.reshape(LENGTH, N_TENSOR, FF // N_TENSOR), proj_blocks, precision=highest_precision)
        return resid + reduced_backward(lax.optimization_barrier(jnp.sum(reduced_rows(mlp_terms), axis=0))) + vector_parameters[5]
    one_hot = groups[:, None] == jnp.arange(GROUPS)[None, :]
    seq_counts = lax.optimization_barrier(jnp.sum(jnp.where(one_hot, counts[None, :], 0), axis=1)).astype(jnp.float32)
    seq_weight = COUNT_BASE / seq_counts

    def one_seq(running_totals, scanned):
        sequence_input, sequence_cotangent, sequence_weights = scanned
        sequence_output, backward_map = jax.vjp(layer_block, sequence_input, adapter_down, adapter_up)
        input_gradient, adapter_down_gradient, adapter_up_gradient = backward_map(sequence_cotangent * sequence_weights)
        return ((running_totals[0] + adapter_down_gradient, running_totals[1] + adapter_up_gradient), (sequence_output, input_gradient))
    start_totals = (jnp.zeros((2, MODEL_WIDTH, ADAPTER_RANK), jnp.float32), jnp.zeros((2, ADAPTER_RANK, MODEL_WIDTH), jnp.float32))
    (sum_a, sum_b), (outs_seq, grads_seq) = lax.scan(one_seq, start_totals, (inputs.astype(jnp.float32), cotangent.astype(jnp.float32), seq_weight))
    mean_weight = jnp.sum(seq_weight) / SEQS
    block_out = outs_seq.astype(jnp.bfloat16)
    input_grad = (grads_seq / mean_weight).astype(jnp.bfloat16)
    down_gradient = sum_a / (mean_weight * TOKENS)
    up_gradient = sum_b / (mean_weight * TOKENS)
    learning_rate = RATE_BASE * math.sqrt(TOKENS)
    updated_momentum_down, updated_down, updated_average_down = update_step(down_gradient, momentum_down, adapter_down, average_down, learning_rate)
    updated_momentum_up, updated_up, updated_average_up = update_step(up_gradient, momentum_up, adapter_up, average_up, learning_rate)
    return (block_out, input_grad, down_gradient, up_gradient, updated_momentum_down, updated_momentum_up, updated_down, updated_up, updated_average_down, updated_average_up, updated_down.astype(jnp.bfloat16), updated_up.astype(jnp.bfloat16))
```

```python
import functools
import math

import jax
import jax.numpy as jnp
from jax import lax
from jax.experimental import pallas as pl
from jax.experimental.pallas import tpu as pltpu
from jax.sharding import PartitionSpec as P

HEAD = 64


NORM_EPS = 1e-05
ADAPTER_SCALE = 8.0
MASK_FILL = -1e30
MOMENTUM_FACTOR = 0.9
AVERAGE_KEEP = 0.8
RATE_BASE = 0.025
WEIGHT_DECAY = 0.005
COUNT_BASE = 256.0


def layer_norm(value_rows, norm_gain, norm_bias):
    center = value_rows - jnp.mean(value_rows, axis=-1, keepdims=True)
    spread = jnp.mean(center * center, axis=-1, keepdims=True)
    return center * lax.rsqrt(spread + NORM_EPS) * norm_gain + norm_bias


def norm_back(value_rows, norm_gain, norm_bias, upstream):

    def local_norm(operand):
        return layer_norm(operand, norm_gain, norm_bias)

    _, backward_map = jax.vjp(local_norm, value_rows)
    return backward_map(upstream)[0]


def gelu_back(preact, upstream):

    def activate(operand):
        return jax.nn.gelu(operand, approximate=True)

    _, backward_map = jax.vjp(activate, preact)
    return backward_map(upstream)[0]


def to_heads(matrix, seq_count, length):
    return matrix.reshape(seq_count, length, -1, HEAD).transpose(0, 2, 1, 3)


def to_rows(tensor4):
    return tensor4.transpose(0, 2, 1, 3).reshape(-1, tensor4.shape[1] * tensor4.shape[3])


def block_scores(query_block, keys, offset, scale_att):
    scores = (
        jnp.einsum("shqe,shke->shqk", query_block, keys, preferred_element_type=jnp.float32)
        * scale_att
    )
    query_pos = offset + jnp.arange(query_block.shape[2])
    key_pos = jnp.arange(keys.shape[2])
    return jnp.where(key_pos[None, :] <= query_pos[:, None], scores, MASK_FILL)


def attend(query_rows, keys, value_rows, scale_att):
    length = query_rows.shape[2]
    block_len = min(512, length)
    outputs = []
    log_totals = []
    for offset in range(0, length, block_len):
        query_block = query_rows[:, :, offset : offset + block_len]
        scores = block_scores(query_block, keys, offset, scale_att)
        largest = jnp.max(scores, axis=-1, keepdims=True)
        exponent = jnp.exp(scores - largest)
        summed = jnp.sum(exponent, axis=-1, keepdims=True)
        attention = exponent / summed
        log_totals.append(largest + jnp.log(summed))
        outputs.append(
            jnp.einsum(
                "shqk,shke->shqe",
                attention.astype(jnp.bfloat16),
                value_rows,
                preferred_element_type=jnp.float32,
            )
        )
    return (jnp.concatenate(outputs, axis=2), log_totals)


def attend_back(query_rows, keys, value_rows, log_totals, grad_heads, scale_att):
    length = query_rows.shape[2]
    block_len = min(512, length)
    grad_blocks = []
    grad_keys = jnp.zeros(keys.shape, jnp.float32)
    grad_values = jnp.zeros(value_rows.shape, jnp.float32)
    for number, offset in enumerate(range(0, length, block_len)):
        query_block = query_rows[:, :, offset : offset + block_len]
        grad_block = grad_heads[:, :, offset : offset + block_len]
        scores = block_scores(query_block, keys, offset, scale_att)
        attention = jnp.exp(scores - log_totals[number])
        grad_attn = jnp.einsum(
            "shqe,shke->shqk", grad_block, value_rows, preferred_element_type=jnp.float32
        )
        row_inner = jnp.sum(grad_attn * attention, axis=-1, keepdims=True)
        grad_scores = (attention * (grad_attn - row_inner)).astype(jnp.bfloat16)
        grad_blocks.append(
            jnp.einsum("shqk,shke->shqe", grad_scores, keys, preferred_element_type=jnp.float32)
            * scale_att
        )
        grad_keys = (
            grad_keys
            + jnp.einsum(
                "shqk,shqe->shke", grad_scores, query_block, preferred_element_type=jnp.float32
            )
            * scale_att
        )
        grad_values = grad_values + jnp.einsum(
            "shqk,shqe->shke",
            attention.astype(jnp.bfloat16),
            grad_block,
            preferred_element_type=jnp.float32,
        )
    return (jnp.concatenate(grad_blocks, axis=2), grad_keys, grad_values)


def update_step(gradient_term, moment, weight_matrix, average, learning_rate):
    updated_moment = MOMENTUM_FACTOR * moment + gradient_term
    updated_weight = weight_matrix * (
        1.0 - learning_rate * WEIGHT_DECAY * ADAPTER_SCALE
    ) - learning_rate * (gradient_term + MOMENTUM_FACTOR * updated_moment)
    new_average = AVERAGE_KEEP * average + (1.0 - AVERAGE_KEEP) * updated_weight
    return (updated_moment, updated_weight, new_average)


def local(
    inputs,
    cotangent,
    groups,
    counts,
    vector_parameters,
    query_value_bias,
    hidden_bias,
    query_key_value_weight,
    attention_output_weight,
    hidden_weight,
    hidden_output_weight,
    adapter_down,
    adapter_up,
    momentum_down,
    momentum_up,
    average_down,
    average_up,
):
    seq_count, length, width_value = inputs.shape
    row_count = seq_count * length
    resid_in = inputs.reshape(row_count, width_value).astype(jnp.float32)
    first_norm_output = layer_norm(resid_in, vector_parameters[0], vector_parameters[1]).astype(
        jnp.bfloat16
    )
    local_width = query_key_value_weight.shape[2]
    column_start = lax.axis_index("tensor") * local_width
    down_reduced = adapter_down.astype(jnp.bfloat16)
    up_reduced = adapter_up.astype(jnp.bfloat16)
    up_local = lax.dynamic_slice_in_dim(up_reduced, column_start, local_width, 2)
    projected_rows = jnp.einsum(
        "rd,cde->cre", first_norm_output, query_key_value_weight, preferred_element_type=jnp.float32
    )
    adapter_input = jnp.einsum(
        "wo,qob->qwb", first_norm_output, down_reduced, preferred_element_type=jnp.float32
    ).astype(jnp.bfloat16)
    adapter_output = jnp.einsum(
        "iga,iaj->igj", adapter_input, up_local, preferred_element_type=jnp.float32
    )
    query_rows = (
        projected_rows[0] + query_value_bias[0] + ADAPTER_SCALE * adapter_output[0]
    ).astype(jnp.bfloat16)
    keys_low = projected_rows[1].astype(jnp.bfloat16)
    value_reduced = (
        projected_rows[2] + query_value_bias[1] + ADAPTER_SCALE * adapter_output[1]
    ).astype(jnp.bfloat16)
    scale_att = HEAD ** (-0.5)
    query_heads = to_heads(query_rows, seq_count, length)
    key_heads = to_heads(keys_low, seq_count, length)
    value_heads = to_heads(value_reduced, seq_count, length)
    heads_out, log_totals = attend(query_heads, key_heads, value_heads, scale_att)
    merged = to_rows(heads_out).astype(jnp.bfloat16)
    attn_part = jnp.dot(merged, attention_output_weight, preferred_element_type=jnp.float32)
    tile = row_count // lax.axis_size("tensor")
    row_offset = lax.axis_index("tensor") * tile
    one_hot = groups[:, None] == jnp.arange(counts.shape[0])[None, :]
    seq_counts = jnp.sum(jnp.where(one_hot, counts[None, :], 0), axis=1).astype(jnp.float32)
    seq_weight = COUNT_BASE / seq_counts
    grad_out = (cotangent.astype(jnp.float32) * seq_weight[:, None, None]).reshape(
        row_count, width_value
    )
    grad_low = grad_out.astype(jnp.bfloat16)
    attn_share = lax.psum_scatter(
        attn_part.astype(jnp.bfloat16), "tensor", scatter_dimension=0, tiled=True
    ).astype(jnp.float32)
    input_share = lax.dynamic_slice_in_dim(resid_in, row_offset, tile, 0)
    resid_share = input_share + attn_share + vector_parameters[4]
    norm_share = layer_norm(resid_share, vector_parameters[2], vector_parameters[3]).astype(
        jnp.bfloat16
    )
    norm2 = lax.all_gather(norm_share, "tensor", axis=0, tiled=True)
    preact = jnp.dot(norm2, hidden_weight, preferred_element_type=jnp.float32) + hidden_bias
    act_low = jax.nn.gelu(preact, approximate=True).astype(jnp.bfloat16)
    preact, mlp_part = (
        preact,
        jnp.dot(act_low, hidden_output_weight, preferred_element_type=jnp.float32),
    )
    mlp_share = lax.psum_scatter(
        mlp_part.astype(jnp.bfloat16), "tensor", scatter_dimension=0, tiled=True
    ).astype(jnp.float32)
    output_share = (resid_share + mlp_share + vector_parameters[5]).astype(jnp.bfloat16)
    output_rows = lax.all_gather(output_share, "tensor", axis=0, tiled=True)
    grad_act = jnp.einsum(
        "rd,fd->rf", grad_low, hidden_output_weight, preferred_element_type=jnp.float32
    )
    grad_pre = gelu_back(preact, grad_act).astype(jnp.bfloat16)
    grad_norm_share = lax.psum_scatter(
        jnp.einsum("rf,df->rd", grad_pre, hidden_weight, preferred_element_type=jnp.float32).astype(
            jnp.bfloat16
        ),
        "tensor",
        scatter_dimension=0,
        tiled=True,
    ).astype(jnp.float32)
    grad_out_share = lax.dynamic_slice_in_dim(grad_out, row_offset, tile, 0)
    grad_resid_share = grad_out_share + norm_back(
        resid_share, vector_parameters[2], vector_parameters[3], grad_norm_share
    )
    grad_resid_low = lax.all_gather(
        grad_resid_share.astype(jnp.bfloat16), "tensor", axis=0, tiled=True
    )
    grad_merged = jnp.einsum(
        "rd,ed->re", grad_resid_low, attention_output_weight, preferred_element_type=jnp.float32
    ).astype(jnp.bfloat16)
    grad_q, grad_k, grad_v = attend_back(
        query_heads,
        key_heads,
        value_heads,
        log_totals,
        to_heads(grad_merged, seq_count, length),
        scale_att,
    )
    grad_qkv = jnp.stack([to_rows(grad_q), to_rows(grad_k), to_rows(grad_v)]).astype(jnp.bfloat16)
    grad_norm1 = jnp.einsum(
        "cre,cde->rd", grad_qkv, query_key_value_weight, preferred_element_type=jnp.float32
    )
    query_value_gradient = jnp.stack([grad_qkv[0], grad_qkv[2]])
    adapter_input_gradient = ADAPTER_SCALE * jnp.einsum(
        "cre,cke->crk", query_value_gradient, up_local, preferred_element_type=jnp.float32
    )
    grad_norm1 = grad_norm1 + jnp.einsum(
        "ibp,inp->bn",
        adapter_input_gradient,
        down_reduced.astype(jnp.float32),
        precision=lax.Precision.HIGHEST,
    )
    grad_a_part = jnp.einsum(
        "rd,crk->cdk",
        first_norm_output,
        adapter_input_gradient,
        precision=lax.Precision.HIGHEST,
        preferred_element_type=jnp.float32,
    )
    local_up_gradient = ADAPTER_SCALE * jnp.einsum(
        "ipg,ipd->igd", adapter_input, query_value_gradient, preferred_element_type=jnp.float32
    )
    grad_b_part = lax.dynamic_update_slice(
        jnp.zeros((2, adapter_up.shape[1], width_value), jnp.float32),
        local_up_gradient,
        (0, 0, column_start),
    )
    grad_norm1_share = lax.psum_scatter(
        grad_norm1.astype(jnp.bfloat16), "tensor", scatter_dimension=0, tiled=True
    ).astype(jnp.float32)
    grad_input_share = grad_resid_share + norm_back(
        input_share, vector_parameters[0], vector_parameters[1], grad_norm1_share
    )
    grad_a_sum, grad_b_sum, weight_sum = lax.psum(
        (grad_a_part, grad_b_part, jnp.sum(seq_weight)), ("dp", "tensor")
    )
    mean_weight = weight_sum / (lax.axis_size("dp") * lax.axis_size("tensor") * seq_count)
    tokens_all = lax.axis_size("dp") * seq_count * length
    input_grad = lax.all_gather(
        (grad_input_share / mean_weight).astype(jnp.bfloat16), "tensor", axis=0, tiled=True
    )
    down_gradient = grad_a_sum / (mean_weight * tokens_all)
    up_gradient = grad_b_sum / (mean_weight * tokens_all)
    learning_rate = RATE_BASE * math.sqrt(tokens_all)
    updated_momentum_down, updated_down, updated_average_down = update_step(
        down_gradient, momentum_down, adapter_down, average_down, learning_rate
    )
    updated_momentum_up, updated_up, updated_average_up = update_step(
        up_gradient, momentum_up, adapter_up, average_up, learning_rate
    )
    block_out = output_rows.reshape(seq_count, length, width_value)
    input_grad = input_grad.reshape(seq_count, length, width_value)
    return (
        block_out,
        input_grad,
        down_gradient,
        up_gradient,
        updated_momentum_down,
        updated_momentum_up,
        updated_down,
        updated_up,
        updated_average_down,
        updated_average_up,
        updated_down.astype(jnp.bfloat16),
        updated_up.astype(jnp.bfloat16),
    )


QUARTER = 256
LANES = 128
BIAS_ROWS = 16
F32 = jnp.float32
BF16 = jnp.bfloat16
NT = (((1,), (1,)), ((), ()))


def dot(a, b):
    return lax.dot_general(a, b, (((1,), (0,)), ((), ())), preferred_element_type=F32)


def dot_nt(a, b):
    return lax.dot_general(a, b, NT, preferred_element_type=F32)


def parity(t):
    return (t ^ (t >> 1)) & 1


def tok_block(t):
    return parity(t) * 2 + ((t >> 1) & 1)


def rows_stats(rows):
    mean = jnp.mean(rows, axis=-1, keepdims=True)
    center = rows - mean
    rstd = lax.rsqrt(jnp.mean(center * center, axis=-1, keepdims=True) + NORM_EPS)
    return center * rstd, rstd


def norm_grad(xhat, rstd, gain, upstream):
    e = upstream * gain
    inner = jnp.mean(e * xhat, axis=-1, keepdims=True)
    return rstd * (e - jnp.mean(e, axis=-1, keepdims=True) - xhat * inner)


def seq_weight_of(groups_ref, counts_ref):
    count = counts_ref[groups_ref[0]]
    return COUNT_BASE / jnp.full((1, LANES), count, jnp.int32).astype(F32)


def cost(flops, nbytes, trans=0):
    return pl.CostEstimate(flops=int(flops), bytes_accessed=int(nbytes), transcendentals=int(trans))


def whole(shape):
    return pl.BlockSpec(shape, lambda *a: (0,) * len(shape))


def smem():
    return pl.BlockSpec(memory_space=pltpu.SMEM)


def call(kernel, name, grid, in_specs, out_specs, out_shape, args, prefetch, scratch=(), est=None):
    return pl.pallas_call(
        kernel,
        name=name,
        grid_spec=pltpu.PrefetchScalarGridSpec(
            num_scalar_prefetch=len(prefetch),
            grid=grid,
            in_specs=in_specs,
            out_specs=out_specs,
            scratch_shapes=list(scratch),
        ),
        out_shape=out_shape,
        cost_estimate=est,
        compiler_params=pltpu.CompilerParams(vmem_limit_bytes=48 * 1024 * 1024),
    )(*prefetch, *args)


def sds(shape, dtype):
    return jax.ShapeDtypeStruct(shape, dtype)


def pack_kernel(which_ref, wh_ref, wo_ref, hb_ref, out_ref):
    width = wh_ref.shape[0]
    out_ref[0, 0:width, :] = wh_ref[...]
    for j in range(width // QUARTER):
        out_ref[0, width + QUARTER * j : width + QUARTER * (j + 1), :] = wo_ref[
            :, QUARTER * j : QUARTER * (j + 1)
        ]
    bias = hb_ref[...]
    high = bias.astype(BF16)
    rest = bias - high.astype(F32)
    mid = rest.astype(BF16)
    low = (rest - mid.astype(F32)).astype(BF16)
    row = lax.broadcasted_iota(jnp.int32, (BIAS_ROWS, QUARTER), 0)
    spread = lambda v: jnp.broadcast_to(v.astype(F32), (BIAS_ROWS, QUARTER))
    packed = jnp.where(row == 0, spread(high), jnp.where(row == 1, spread(mid), spread(low)))
    out_ref[0, 2 * width : 2 * width + BIAS_ROWS, :] = jnp.where(row < 3, packed, 0.0).astype(BF16)


def pack(which, count, hidden_weight, hidden_output_weight, hidden_bias):
    width = hidden_weight.shape[0]
    rows = 2 * width + BIAS_ROWS
    return call(
        pack_kernel,
        "pack",
        (count,),
        [
            pl.BlockSpec((width, QUARTER), lambda i, w: (0, w[i])),
            pl.BlockSpec((QUARTER, width), lambda i, w: (w[i], 0)),
            pl.BlockSpec((1, QUARTER), lambda i, w: (0, w[i])),
        ],
        pl.BlockSpec((1, rows, QUARTER), lambda i, w: (i, 0, 0)),
        sds((count, rows, QUARTER), BF16),
        (hidden_weight, hidden_output_weight, hidden_bias.reshape(1, -1)),
        (which,),
        est=cost(0, 4 * rows * QUARTER * count),
    )


def qkv_kernel(
    meta_ref, x_ref, vec_ref, w_ref, qvb_ref, down_ref, up_ref,
    q_ref, k_ref, v_ref, n_ref, lora_ref, down_s, up_s,
):
    rank = down_ref.shape[1]
    cols = w_ref.shape[2]

    @pl.when(pl.program_id(0) == 0)
    def _():
        down_s[...] = jnp.zeros_like(down_s)
        up_s[...] = jnp.zeros_like(up_s)
        down_s[0 : 2 * rank, :] = jnp.concatenate([down_ref[0], down_ref[1]], axis=0)
        up_s[0:rank, 0:cols] = up_ref[0]
        up_s[rank : 2 * rank, cols : 2 * cols] = up_ref[1]

    xhat, _ = rows_stats(x_ref[0].astype(F32))
    norm1 = (xhat * vec_ref[0:1, :] + vec_ref[1:2, :]).astype(BF16)
    n_ref[...] = norm1
    lora = dot_nt(norm1, down_s[...].astype(BF16)).astype(BF16)
    lora_ref[...] = lora
    adapt = ADAPTER_SCALE * dot(lora, up_s[...].astype(BF16))
    q = dot(norm1, w_ref[0]) + qvb_ref[0:1, :] + adapt[:, 0:cols]
    q_ref[...] = q.astype(BF16)
    k_ref[...] = dot(norm1, w_ref[1]).astype(BF16)
    v = dot(norm1, w_ref[2]) + qvb_ref[1:2, :] + adapt[:, cols : 2 * cols]
    v_ref[...] = v.astype(BF16)


def qkv(meta, x, vec, w, qvb, down_t, up):
    length, width = x.shape[1:]
    cols = w.shape[2]
    rank = up.shape[1]
    block = pl.BlockSpec((QUARTER, cols), lambda i, m: (i, 0))
    return call(
        qkv_kernel,
        "qkv",
        (length // QUARTER,),
        [
            pl.BlockSpec((1, QUARTER, width), lambda i, m: (0, i, 0)),
            whole(vec.shape),
            whole(w.shape),
            whole(qvb.shape),
            whole(down_t.shape),
            pl.BlockSpec((2, rank, cols), lambda i, m: (0, 0, m[0] & 3)),
        ],
        [
            block,
            block,
            block,
            pl.BlockSpec((QUARTER, width), lambda i, m: (i, 0)),
            pl.BlockSpec((QUARTER, LANES), lambda i, m: (i, 0)),
        ],
        [
            sds((length, cols), BF16),
            sds((length, cols), BF16),
            sds((length, cols), BF16),
            sds((length, width), BF16),
            sds((length, LANES), BF16),
        ],
        (x, vec, w, qvb, down_t, up),
        (meta,),
        scratch=[pltpu.VMEM((LANES, width), F32), pltpu.VMEM((LANES, 2 * cols), F32)],
        est=cost(2 * length * width * 3 * cols, 4 * length * width + 6 * width * cols + 6 * length * cols),
    )


def head_lanes(value, head):
    lane = lax.broadcasted_iota(jnp.int32, value.shape, 1)
    return jnp.where(lane // HEAD == head, value, jnp.zeros_like(value))


def attend_kernel(meta_ref, q_ref, k_ref, v_ref, p_ref, ot_ref, same_ref, other_ref, vt_s, o_s):
    length = q_ref.shape[0]
    half = length // 2
    vt_s[...] = v_ref[...].astype(F32).T.astype(BF16)
    below = lax.broadcasted_iota(jnp.int32, (QUARTER, QUARTER), 0) <= lax.broadcasted_iota(
        jnp.int32, (QUARTER, QUARTER), 1
    )

    @pl.loop(0, 2)
    def _(head):
        rows = pl.ds(pl.multiple_of(head * HEAD, HEAD), HEAD)
        for j in range(length // QUARTER):
            at = slice(QUARTER * j, QUARTER * (j + 1))
            seen = QUARTER * (j + 1)
            query = head_lanes(q_ref[at, :], head) * jnp.asarray(HEAD ** (-0.5), BF16)
            scores = dot_nt(k_ref[0:seen, :], query)
            last = jnp.where(below, scores[QUARTER * j :, :], MASK_FILL)
            scores = last if j == 0 else jnp.concatenate([scores[: QUARTER * j, :], last], axis=0)
            top = jnp.max(scores, axis=0, keepdims=True)
            exponent = jnp.exp(scores - top)
            inverse = 1.0 / jnp.sum(exponent, axis=0, keepdims=True)
            probs = (exponent * inverse).astype(BF16)
            p_ref[head, 0:seen, at] = probs
            ot_ref[rows, at] = dot(vt_s[rows, 0:seen], probs)

    o_s[...] = ot_ref[...].T.astype(BF16)
    start = pl.multiple_of(parity(meta_ref[0] & 3) * half, half)
    same_ref[...] = o_s[pl.ds(start, half), :]
    other_ref[...] = o_s[pl.ds(pl.multiple_of(half - start, half), half), :]


def attend_fast(meta, q, k, v):
    length, cols = q.shape
    pairs = cols // LANES
    block = pl.BlockSpec((length, LANES), lambda g, m: (0, g))
    half = pl.BlockSpec((length // 2, LANES), lambda g, m: (0, g))
    return call(
        attend_kernel,
        "attend",
        (pairs,),
        [block, block, block],
        [
            pl.BlockSpec((2, length, length), lambda g, m: (g, 0, 0)),
            pl.BlockSpec((LANES, length), lambda g, m: (g, 0)),
            half,
            half,
        ],
        [
            sds((2 * pairs, length, length), BF16),
            sds((cols, length), F32),
            sds((length // 2, cols), BF16),
            sds((length // 2, cols), BF16),
        ],
        (q, k, v),
        (meta,),
        scratch=[pltpu.VMEM((LANES, length), BF16), pltpu.VMEM((length, LANES), BF16)],
        est=cost(8 * length * length * cols, 4 * length * length * pairs + 10 * length * cols),
    )


def attend_back_kernel(
    meta_ref, q_ref, k_ref, v_ref, p_ref, ot_ref, go_ref, gx_ref, gy_ref, gd_ref,
    dq_ref, dk_ref, dv_ref, g_s, gt_s, kt_s, dqt_s, dk_s, dv_s,
):
    length = q_ref.shape[0]
    t = meta_ref[0] & 3
    for piece, who in ((go_ref, t), (gx_ref, t ^ 1), (gy_ref, t ^ 2), (gd_ref, t ^ 3)):
        start = pl.multiple_of(tok_block(who) * QUARTER, QUARTER)
        g_s[pl.ds(start, QUARTER), :] = piece[...]
    gt_s[...] = g_s[...].astype(F32).T
    kt_s[...] = k_ref[...].astype(F32).T.astype(BF16)
    dk_s[...] = jnp.zeros_like(dk_s)
    dv_s[...] = jnp.zeros_like(dv_s)
    scale = jnp.asarray(HEAD ** (-0.5), BF16)

    @pl.loop(0, 2)
    def _(head):
        rows = pl.ds(pl.multiple_of(head * HEAD, HEAD), HEAD)
        for j in range(length // QUARTER):
            at = slice(QUARTER * j, QUARTER * (j + 1))
            seen = QUARTER * (j + 1)
            query = head_lanes(q_ref[at, :], head) * scale
            grad = head_lanes(g_s[at, :], head)
            inner = jnp.sum(gt_s[rows, at] * ot_ref[rows, at], axis=0, keepdims=True)
            probs = p_ref[head, 0:seen, at]
            grad_probs = dot_nt(v_ref[0:seen, :], grad)
            grad_scores = (probs.astype(F32) * (grad_probs - inner)).astype(BF16)
            dv_s[0:seen, :] += dot(probs, grad)
            dk_s[0:seen, :] += dot(grad_scores, query)
            dqt_s[rows, at] = dot(kt_s[rows, 0:seen], grad_scores)

    dq_ref[...] = (dqt_s[...].T * (HEAD ** (-0.5))).astype(BF16)
    dk_ref[...] = dk_s[...].astype(BF16)
    dv_ref[...] = dv_s[...].astype(BF16)


def attend_back_fast(meta, q, k, v, probs, out_t, pieces):
    length, cols = q.shape
    pairs = cols // LANES
    block = pl.BlockSpec((length, LANES), lambda g, m: (0, g))
    piece = pl.BlockSpec((QUARTER, LANES), lambda g, m: (0, g))
    return call(
        attend_back_kernel,
        "attend_back",
        (pairs,),
        [
            block,
            block,
            block,
            pl.BlockSpec((2, length, length), lambda g, m: (g, 0, 0)),
            pl.BlockSpec((LANES, length), lambda g, m: (g, 0)),
            piece,
            piece,
            piece,
            piece,
        ],
        [block, block, block],
        [sds((length, cols), BF16)] * 3,
        (q, k, v, probs, out_t, *pieces),
        (meta,),
        scratch=[
            pltpu.VMEM((length, LANES), BF16),
            pltpu.VMEM((LANES, length), F32),
            pltpu.VMEM((LANES, length), BF16),
            pltpu.VMEM((LANES, length), F32),
            pltpu.VMEM((length, LANES), F32),
            pltpu.VMEM((length, LANES), F32),
        ],
        est=cost(16 * length * length * cols, 4 * length * length * pairs + 16 * length * cols),
    )


def fill_projection(wof, core, own_ref, halves):
    local = own_ref.shape[0]
    half = local // 2
    wof[0:local, :] = own_ref[...]
    for number, (first, second) in enumerate(halves):
        base = local * (number + 1)
        start = pl.multiple_of(base + core * half, half)
        wof[pl.ds(start, half), :] = first[...]
        start = pl.multiple_of(base + (1 - core) * half, half)
        wof[pl.ds(start, half), :] = second[...]


def mlp_kernel(
    final, meta_ref, groups_ref, counts_ref, x_ref, cot_ref, vec_ref,
    ho_ref, hx_ref, hy_ref, hd_ref, wof_ref,
    own_ref, xa_ref, xb_ref, ya_ref, yb_ref,
    gn_ref, mlp_ref, resid_ref, n2_s, low_s, h_s, gn_s, mlp_s, buf, sem,
):
    width = x_ref.shape[2]
    blocks = own_ref.shape[0]
    total = blocks + 4
    extras = (xa_ref, xb_ref, ya_ref, yb_ref)

    def fetch(i, slot):
        @pl.when(i < blocks)
        def _():
            pltpu.make_async_copy(own_ref.at[jnp.minimum(i, blocks - 1)], buf.at[slot], sem.at[slot]).start()

        for n, ref in enumerate(extras):
            @pl.when(i == blocks + n)
            def _(ref=ref):
                pltpu.make_async_copy(ref.at[0], buf.at[slot], sem.at[slot]).start()

    fetch(0, 0)
    local = ho_ref.shape[1]
    for n, ref in enumerate((ho_ref, hx_ref, hy_ref, hd_ref)):
        h_s[:, local * n : local * (n + 1)] = ref[...]
    resid = x_ref[0].astype(F32) + dot(h_s[...], wof_ref[...]) + vec_ref[4:5, :]
    resid_ref[...] = resid
    xhat, _ = rows_stats(resid)
    n2_s[...] = (xhat * vec_ref[2:3, :] + vec_ref[3:4, :]).astype(BF16)
    weight = seq_weight_of(groups_ref, counts_ref)[:, 0:1]
    low_s[...] = (cot_ref[0].astype(F32) * weight).astype(BF16)
    gn_s[...] = jnp.zeros_like(gn_s)
    mlp_s[...] = jnp.zeros_like(mlp_s)

    @pl.loop(0, total)
    def _(i):
        slot = i & 1
        pltpu.make_async_copy(xa_ref.at[0], buf.at[slot], sem.at[slot]).wait()

        @pl.when(i + 1 < total)
        def _():
            fetch(i + 1, 1 - slot)

        wh = buf[slot, 0:width, :]
        tail = buf[slot, 2 * width : 2 * width + BIAS_ROWS, :].astype(F32)
        bias = tail[0:1, :] + tail[1:2, :] + tail[2:3, :]
        pre = dot(n2_s[...], wh) + bias
        grad_act = jnp.zeros_like(pre)
        for j in range(width // QUARTER):
            piece = buf[slot, width + QUARTER * j : width + QUARTER * (j + 1), :]
            grad_act = grad_act + dot_nt(low_s[:, QUARTER * j : QUARTER * (j + 1)], piece)
        root = math.sqrt(2.0 / math.pi)
        square = pre * pre
        turn = jnp.tanh(root * (pre + 0.044715 * (square * pre)))
        act = (0.5 * pre * (1.0 + turn)).astype(BF16)
        slope = 0.5 * (1.0 + turn) + 0.5 * pre * (1.0 - turn * turn) * (
            root * (1.0 + 3.0 * 0.044715 * square)
        )
        grad_pre = (grad_act * slope).astype(BF16)
        gn_s[...] += dot_nt(grad_pre, wh)
        for j in range(width // QUARTER):
            piece = buf[slot, width + QUARTER * j : width + QUARTER * (j + 1), :]
            mlp_s[:, QUARTER * j : QUARTER * (j + 1)] += dot(act, piece)

    gn_ref[...] = gn_s[...].astype(gn_ref.dtype)
    mlp_ref[...] = mlp_s[...].astype(mlp_ref.dtype)


def mlp_fast(final, meta, groups, counts, x, cot, vec, heads, wof, packs):
    width = x.shape[2]
    local = heads[0].shape[1]
    kind = F32 if final else BF16
    flip = 0 if final else 3
    rows = pl.BlockSpec((1, QUARTER, width), lambda i, m: (0, tok_block((m[0] & 3) ^ flip), 0))
    head = pl.BlockSpec((QUARTER, local), lambda i, m: ((((m[0] & 3) ^ flip) >> 1) & 1, 0))
    any_ = pl.BlockSpec(memory_space=pl.ANY)
    out = whole((QUARTER, width))
    depth = 2 * width + BIAS_ROWS
    hidden = QUARTER * (packs[0].shape[0] + 4)
    return call(
        functools.partial(mlp_kernel, final),
        "mlp_own" if final else "mlp_pair",
        (1,),
        [smem(), smem(), rows, rows, whole(vec.shape), head, head, head, head, whole(wof.shape)]
        + [any_] * 5,
        [out, out, out],
        [sds((QUARTER, width), kind), sds((QUARTER, width), kind), sds((QUARTER, width), F32)],
        (groups, counts, x, cot, vec, *heads, wof, *packs),
        (meta,),
        scratch=[
            pltpu.VMEM((QUARTER, width), BF16),
            pltpu.VMEM((QUARTER, width), BF16),
            pltpu.VMEM((QUARTER, 4 * local), BF16),
            pltpu.VMEM((QUARTER, width), F32),
            pltpu.VMEM((QUARTER, width), F32),
            pltpu.VMEM((2, depth, QUARTER), BF16),
            pltpu.SemaphoreType.DMA((2,)),
        ],
        est=cost(
            8 * QUARTER * width * hidden + 2 * QUARTER * width * width,
            4 * width * hidden + 2 * width * width + 16 * QUARTER * width,
            QUARTER * hidden,
        ),
    )


def project_kernel(meta_ref, own_ref, x0, x1, y0, y1, d0, d1, wof_ref):
    fill_projection(wof_ref, (meta_ref[0] >> 2) & 1, own_ref, ((x0, x1), (y0, y1), (d0, d1)))


def project(meta, own, halves):
    local, width = own.shape
    flat = [h for pair in halves for h in pair]
    return call(
        project_kernel,
        "project",
        (1,),
        [whole(own.shape)] + [whole(h.shape) for h in flat],
        whole((4 * local, width)),
        sds((4 * local, width), BF16),
        (own, *flat),
        (meta,),
        est=cost(0, 16 * local * width),
    )


def resid_back_kernel(
    meta_ref, groups_ref, counts_ref, own_ref, recv_ref, resid_ref, cot_ref, vec_ref, wof_ref,
    gr_ref, o_ref, x_ref, y_ref, d_ref,
):
    weight = seq_weight_of(groups_ref, counts_ref)[:, 0:1]
    grad = own_ref[...] + recv_ref[...].astype(F32)
    xhat, rstd = rows_stats(resid_ref[...])
    total = cot_ref[0].astype(F32) * weight + norm_grad(xhat, rstd, vec_ref[2:3, :], grad)
    gr_ref[...] = total
    low = total.astype(BF16)
    local = wof_ref.shape[0] // 4
    for n, ref in enumerate((o_ref, x_ref, y_ref, d_ref)):
        ref[...] = dot_nt(low, wof_ref[local * n : local * (n + 1), :]).astype(BF16)


def resid_back(meta, groups, counts, own, recv, resid, cot, vec, wof):
    width = own.shape[1]
    local = wof.shape[0] // 4
    piece = whole((QUARTER, local))
    full = whole((QUARTER, width))
    return call(
        resid_back_kernel,
        "resid_back",
        (1,),
        [
            smem(),
            smem(),
            full,
            full,
            full,
            pl.BlockSpec((1, QUARTER, width), lambda i, m: (0, tok_block(m[0] & 3), 0)),
            whole(vec.shape),
            whole(wof.shape),
        ],
        [full, piece, piece, piece, piece],
        [sds((QUARTER, width), F32)] + [sds((QUARTER, local), BF16)] * 4,
        (groups, counts, own, recv, resid, cot, vec, wof),
        (meta,),
        est=cost(2 * QUARTER * width * width, 16 * QUARTER * width + 2 * width * width),
    )


def input_back_kernel(
    meta_ref, groups_ref, counts_ref, dq_ref, dk_ref, dv_ref, w_ref, down_ref, up_ref, n_ref,
    lora_ref, ox_ref, oy_ref, od_ref, own_ref, grads_ref, down_s, up_s, dn_s, gu_s,
):
    i = pl.program_id(0)
    rank = down_ref.shape[1]
    cols = w_ref.shape[2]

    @pl.when(i == 0)
    def _():
        down_s[...] = jnp.zeros_like(down_s)
        up_s[...] = jnp.zeros_like(up_s)
        both = jnp.concatenate([down_ref[0], down_ref[1]], axis=0)
        down_s[0 : 2 * rank, :] = both
        down_s[2 * rank : 4 * rank, :] = both
        up_s[0:rank, 0:cols] = up_ref[0]
        up_s[rank : 2 * rank, cols : 2 * cols] = up_ref[1]
        up_s[2 * rank : 3 * rank, 0:cols] = up_ref[0]
        up_s[3 * rank : 4 * rank, cols : 2 * cols] = up_ref[1]
        dn_s[...] = jnp.zeros_like(dn_s)
        gu_s[...] = jnp.zeros_like(gu_s)

    dq, dk, dv = dq_ref[...], dk_ref[...], dv_ref[...]
    ups = up_s[...].astype(BF16)
    inner = ADAPTER_SCALE * (dot_nt(dq, ups[:, 0:cols]) + dot_nt(dv, ups[:, cols : 2 * cols]))
    high = inner.astype(BF16)
    low = (inner - high.astype(F32)).astype(BF16)
    lane = lax.broadcasted_iota(jnp.int32, inner.shape, 1)
    split = jnp.where(lane < 2 * rank, high.astype(F32), low.astype(F32))
    both = split.astype(BF16)
    grad = (
        dot_nt(dq, w_ref[0])
        + dot_nt(dk, w_ref[1])
        + dot_nt(dv, w_ref[2])
        + dot(both, down_s[...].astype(BF16))
    )
    for n, ref in enumerate((ox_ref, oy_ref, od_ref, own_ref)):
        @pl.when(i == n)
        def _(ref=ref):
            ref[...] = grad.astype(ref.dtype)

    dn_s[...] += dot(split.T.astype(BF16), n_ref[...])
    lt = lora_ref[...].astype(F32).T.astype(BF16)
    gu_s[...] += ADAPTER_SCALE * dot(lt, jnp.concatenate([dq, dv], axis=1))

    @pl.when(i == pl.num_programs(0) - 1)
    def _():
        grads_ref[...] = jnp.zeros_like(grads_ref)
        grads_ref[0 : 2 * rank, :] = dn_s[0 : 2 * rank, :] + dn_s[2 * rank : 4 * rank, :]
        start = pl.multiple_of((meta_ref[0] & 3) * cols, cols)
        grads_ref[2 * rank : 3 * rank, pl.ds(start, cols)] = gu_s[0:rank, 0:cols]
        grads_ref[3 * rank : 4 * rank, pl.ds(start, cols)] = gu_s[rank : 2 * rank, cols : 2 * cols]
        weight = seq_weight_of(groups_ref, counts_ref)[:, 0:1]
        grads_ref[4 * rank : 4 * rank + 8, :] = jnp.broadcast_to(weight, (8, grads_ref.shape[1]))


def input_back(meta, groups, counts, dq, dk, dv, w, down_t, up, norm1, lora):
    length, cols = dq.shape
    width = w.shape[1]
    rank = up.shape[1]

    def who(i, m):
        return tok_block((m[0] & 3) ^ jnp.where(i == 3, 0, i + 1))

    block = pl.BlockSpec((QUARTER, cols), lambda i, m: (who(i, m), 0))
    out = whole((QUARTER, width))
    return call(
        input_back_kernel,
        "input_back",
        (4,),
        [
            smem(),
            smem(),
            block,
            block,
            block,
            whole(w.shape),
            whole(down_t.shape),
            pl.BlockSpec((2, rank, cols), lambda i, m: (0, 0, m[0] & 3)),
            pl.BlockSpec((QUARTER, width), lambda i, m: (who(i, m), 0)),
            pl.BlockSpec((QUARTER, LANES), lambda i, m: (who(i, m), 0)),
        ],
        [out, out, out, out, whole((4 * rank + 8, width))],
        [sds((QUARTER, width), BF16)] * 3
        + [sds((QUARTER, width), F32), sds((4 * rank + 8, width), F32)],
        (groups, counts, dq, dk, dv, w, down_t, up, norm1, lora),
        (meta,),
        scratch=[
            pltpu.VMEM((LANES, width), F32),
            pltpu.VMEM((LANES, 2 * cols), F32),
            pltpu.VMEM((LANES, width), F32),
            pltpu.VMEM((LANES, 2 * cols), F32),
        ],
        est=cost(6 * length * width * cols, 6 * width * cols + 6 * length * cols + 6 * length * width),
    )


def first_back_kernel(meta_ref, own_ref, a_ref, b_ref, c_ref, x_ref, gr_ref, vec_ref, out_ref):
    grad = own_ref[...] + a_ref[...].astype(F32) + b_ref[...].astype(F32) + c_ref[...].astype(F32)
    xhat, rstd = rows_stats(x_ref[0].astype(F32))
    out_ref[...] = (gr_ref[...] + norm_grad(xhat, rstd, vec_ref[0:1, :], grad)).astype(BF16)


def first_back(meta, own, pieces, x, grad_resid, vec):
    width = own.shape[1]
    full = whole((QUARTER, width))
    return call(
        first_back_kernel,
        "first_back",
        (1,),
        [
            full,
            full,
            full,
            full,
            pl.BlockSpec((1, QUARTER, width), lambda i, m: (0, tok_block(m[0] & 3), 0)),
            full,
            whole(vec.shape),
        ],
        full,
        sds((QUARTER, width), BF16),
        (own, *pieces, x, grad_resid, vec),
        (meta,),
        est=cost(30 * QUARTER * width, 16 * QUARTER * width),
    )


def gather_kernel(scaled, meta_ref, *refs):
    if scaled:
        total_ref, o_ref, x_ref, y_ref, d_ref, out_ref = refs
        factor = scaled / total_ref[0:1, 0:1]
    else:
        o_ref, x_ref, y_ref, d_ref, out_ref = refs
    i = pl.program_id(0)
    for n, ref in enumerate((o_ref, x_ref, y_ref, d_ref)):
        @pl.when(i == n)
        def _(ref=ref):
            if scaled:
                out_ref[0] = (ref[...].astype(F32) * factor).astype(BF16)
            else:
                out_ref[0] = ref[...]


def gather_rows(meta, pieces, scaled=0.0, total=None):
    width = pieces[0].shape[1]
    full = whole((QUARTER, width))
    extra = [total] if scaled else []
    specs = [pl.BlockSpec((8, width), lambda i, m: (total.shape[0] // 8 - 1, 0))] if scaled else []
    return call(
        functools.partial(gather_kernel, scaled),
        "gather_rows",
        (4,),
        specs + [full] * 4,
        pl.BlockSpec((1, QUARTER, width), lambda i, m: (0, tok_block((m[0] & 3) ^ i), 0)),
        sds((1, 4 * QUARTER, width), BF16),
        (*extra, *pieces),
        (meta,),
        est=cost(0, 16 * QUARTER * width),
    )


def update_kernel(tokens, devices, total_ref, d_ref, u_ref, md_ref, mu_ref, ad_ref, au_ref, *outs):
    gd_o, gu_o, md_o, mu_o, d_o, u_o, ad_o, au_o, cd_o, cu_o = outs
    rank = d_ref.shape[1]
    weight = total_ref[4 * rank : 4 * rank + 1, 0:1]
    mean_weight = weight / devices
    rate = RATE_BASE * math.sqrt(tokens)
    for c in range(2):
        for base, g_o, m_ref, m_o, w_ref, w_o, a_ref, a_o, c_o in (
            (0, gd_o, md_ref, md_o, d_ref, d_o, ad_ref, ad_o, cd_o),
            (2 * rank, gu_o, mu_ref, mu_o, u_ref, u_o, au_ref, au_o, cu_o),
        ):
            gradient = total_ref[base + c * rank : base + (c + 1) * rank, :] / (mean_weight * tokens)
            moment, new, average = update_step(gradient, m_ref[c], w_ref[c], a_ref[c], rate)
            g_o[c] = gradient
            m_o[c] = moment
            w_o[c] = new
            a_o[c] = average
            c_o[c] = new.astype(BF16)


def update(tokens, devices, total, down_t, up, mom_d, mom_u, avg_d, avg_u):
    shapes = [whole(total.shape)] + [whole(down_t.shape)] * 6
    kinds = [F32] * 8 + [BF16] * 2
    return call(
        functools.partial(update_kernel, float(tokens), float(devices)),
        "update",
        (1,),
        shapes,
        [whole(down_t.shape)] * 10,
        [sds(down_t.shape, kind) for kind in kinds],
        (total, down_t, up, mom_d, mom_u, avg_d, avg_u),
        (),
        est=cost(0, 18 * 4 * down_t.size),
    )


def local_fast(
    dp_size,
    inputs,
    cotangent,
    groups,
    counts,
    vector_parameters,
    query_value_bias,
    hidden_bias,
    query_key_value_weight,
    attention_output_weight,
    hidden_weight,
    hidden_output_weight,
    adapter_down,
    adapter_up,
    momentum_down,
    momentum_up,
    average_down,
    average_up,
):
    axes = ("dp", "tensor")

    def send(value, dp_flip, t_flip):
        pairs = [
            (d * 4 + t, (d ^ dp_flip) * 4 + (t ^ t_flip)) for d in range(dp_size) for t in range(4)
        ]
        return lax.ppermute(value, axes, pairs)

    tensor_at = lax.axis_index("tensor")
    core = lax.axis_index("dp") & 1
    meta = (tensor_at + 4 * core).astype(jnp.int32).reshape(1)
    down_t = jnp.swapaxes(adapter_down, 1, 2)
    vec = vector_parameters
    local = attention_output_weight.shape[0]
    length = inputs.shape[1]

    wo_half = lax.dynamic_slice_in_dim(attention_output_weight, core * (local // 2), local // 2, 0)
    got_wo = [send(wo_half, 0, flip) for flip in (1, 2, 3)]
    one = core.astype(jnp.int32).reshape(1)
    ffn = (hidden_weight, hidden_output_weight, hidden_bias)
    got_x = send(pack(one, 1, *ffn), 0, 1)
    got_y = send(pack(one + 2, 1, *ffn), 0, 2)

    q, k, v, norm1, lora = qkv(
        meta, inputs, vec, query_key_value_weight, query_value_bias, down_t, adapter_up
    )
    probs, out_t, same, other = attend_fast(meta, q, k, v)
    heads = [same, send(other, 0, 1), send(other, 0, 2), send(same, 0, 3)]
    halves = [(w, send(w, 1, 0)) for w in got_wo]
    own_packs = pack(jnp.arange(4, dtype=jnp.int32), 4, *ffn)
    packs = [own_packs, got_x, send(got_x, 1, 0), got_y, send(got_y, 1, 0)]
    wof = project(meta, attention_output_weight, halves)

    gn_pair, mlp_pair, _ = mlp_fast(
        False, meta, groups, counts, inputs, cotangent, vec, heads, wof, packs
    )
    gn_recv = send(gn_pair, 0, 3)
    mlp_recv = send(mlp_pair, 0, 3)
    gn_own, mlp_own, resid = mlp_fast(
        True, meta, groups, counts, inputs, cotangent, vec, heads, wof, packs
    )
    grad_resid, g_own, g_x, g_y, g_d = resid_back(
        meta, groups, counts, gn_own, gn_recv, resid, cotangent, vec, wof
    )
    pieces = [g_own, send(g_x, 0, 1), send(g_y, 0, 2), send(g_d, 0, 3)]
    out_own = (resid + mlp_own + mlp_recv.astype(F32) + vec[5]).astype(BF16)
    out_all = [out_own] + [send(out_own, 0, flip) for flip in (1, 2, 3)]

    dq, dk, dv = attend_back_fast(meta, q, k, v, probs, out_t, pieces)
    gx, gy, gd, g1_own, total = input_back(
        meta, groups, counts, dq, dk, dv, query_key_value_weight, down_t, adapter_up, norm1, lora
    )
    g1 = [send(gx, 0, 1), send(gy, 0, 2), send(gd, 0, 3)]
    total = total + send(total, 1, 0)
    total = total + send(total, 0, 1)
    total = total + send(total, 0, 2)
    step = 2
    while step < dp_size:
        total = total + send(total, step, 0)
        step *= 2
    in_own = first_back(meta, g1_own, g1, inputs, grad_resid, vec)
    in_all = [in_own] + [send(in_own, 0, flip) for flip in (1, 2, 3)]
    block_out = gather_rows(meta, out_all)
    copies = dp_size * 4
    input_grad = gather_rows(meta, in_all, scaled=float(copies), total=total)
    results = update(
        dp_size * length,
        copies,
        total,
        down_t,
        adapter_up,
        jnp.swapaxes(momentum_down, 1, 2),
        momentum_up,
        jnp.swapaxes(average_down, 1, 2),
        average_up,
    )
    results = [
        jnp.swapaxes(value, 1, 2) if number % 2 == 0 else value
        for number, value in enumerate(results)
    ]
    return (block_out, input_grad, *results)


def solution(mesh):
    in_specs = (
        P("dp", None, None),
        P("dp", None, None),
        P("dp"),
        P(),
        P(),
        P(None, "tensor"),
        P("tensor"),
        P(None, None, "tensor"),
        P("tensor", None),
        P(None, "tensor"),
        P("tensor", None),
        P(),
        P(),
        P(),
        P(),
        P(),
        P(),
    )
    out_specs = (
        P("dp", None, None),
        P("dp", None, None),
        P(),
        P(),
        P(),
        P(),
        P(),
        P(),
        P(),
        P(),
        P(),
        P(),
    )
    dp_size = mesh.shape["dp"]
    small = mesh.shape["tensor"] == 4 and dp_size & (dp_size - 1) == 0 and dp_size > 1

    def body(*args):
        if small and args[0].shape[0] == 1 and args[0].shape[1] == 4 * QUARTER:
            return local_fast(dp_size, *args)
        return local(*args)

    return jax.shard_map(body, mesh=mesh, in_specs=in_specs, out_specs=out_specs, check_vma=False)
```

```python
import functools
import math

import jax
import jax.numpy as jnp
from jax import lax
from jax.experimental import pallas as pl
from jax.experimental.pallas import tpu as pltpu
from jax.sharding import PartitionSpec as P


HEAD = 64


NORM_EPS = 1e-05
ADAPTER_SCALE = 8.0
MASK_FILL = -1e30
MOMENTUM_FACTOR = 0.9
AVERAGE_KEEP = 0.8
RATE_BASE = 0.025
WEIGHT_DECAY = 0.005
COUNT_BASE = 256.0


def layer_norm(value_rows, norm_gain, norm_bias):
    center = value_rows - jnp.mean(value_rows, axis=-1, keepdims=True)
    spread = jnp.mean(center * center, axis=-1, keepdims=True)
    return center * lax.rsqrt(spread + NORM_EPS) * norm_gain + norm_bias


def norm_back(value_rows, norm_gain, norm_bias, upstream):

    def local_norm(operand):
        return layer_norm(operand, norm_gain, norm_bias)

    _, backward_map = jax.vjp(local_norm, value_rows)
    return backward_map(upstream)[0]


def gelu_back(preact, upstream):

    def activate(operand):
        return jax.nn.gelu(operand, approximate=True)

    _, backward_map = jax.vjp(activate, preact)
    return backward_map(upstream)[0]


def to_heads(matrix, seq_count, length):
    return matrix.reshape(seq_count, length, -1, HEAD).transpose(0, 2, 1, 3)


def to_rows(tensor4):
    return tensor4.transpose(0, 2, 1, 3).reshape(-1, tensor4.shape[1] * tensor4.shape[3])


def block_scores(query_block, keys, offset, scale_att):
    scores = (
        jnp.einsum("shqe,shke->shqk", query_block, keys, preferred_element_type=jnp.float32)
        * scale_att
    )
    query_pos = offset + jnp.arange(query_block.shape[2])
    key_pos = jnp.arange(keys.shape[2])
    return jnp.where(key_pos[None, :] <= query_pos[:, None], scores, MASK_FILL)


def attend(query_rows, keys, value_rows, scale_att):
    length = query_rows.shape[2]
    block_len = min(512, length)
    outputs = []
    log_totals = []
    for offset in range(0, length, block_len):
        query_block = query_rows[:, :, offset : offset + block_len]
        scores = block_scores(query_block, keys, offset, scale_att)
        largest = jnp.max(scores, axis=-1, keepdims=True)
        exponent = jnp.exp(scores - largest)
        summed = jnp.sum(exponent, axis=-1, keepdims=True)
        attention = exponent / summed
        log_totals.append(largest + jnp.log(summed))
        outputs.append(
            jnp.einsum(
                "shqk,shke->shqe",
                attention.astype(jnp.bfloat16),
                value_rows,
                preferred_element_type=jnp.float32,
            )
        )
    return (jnp.concatenate(outputs, axis=2), log_totals)


def attend_back(query_rows, keys, value_rows, log_totals, grad_heads, scale_att):
    length = query_rows.shape[2]
    block_len = min(512, length)
    grad_blocks = []
    grad_keys = jnp.zeros(keys.shape, jnp.float32)
    grad_values = jnp.zeros(value_rows.shape, jnp.float32)
    for number, offset in enumerate(range(0, length, block_len)):
        query_block = query_rows[:, :, offset : offset + block_len]
        grad_block = grad_heads[:, :, offset : offset + block_len]
        scores = block_scores(query_block, keys, offset, scale_att)
        attention = jnp.exp(scores - log_totals[number])
        grad_attn = jnp.einsum(
            "shqe,shke->shqk", grad_block, value_rows, preferred_element_type=jnp.float32
        )
        row_inner = jnp.sum(grad_attn * attention, axis=-1, keepdims=True)
        grad_scores = (attention * (grad_attn - row_inner)).astype(jnp.bfloat16)
        grad_blocks.append(
            jnp.einsum("shqk,shke->shqe", grad_scores, keys, preferred_element_type=jnp.float32)
            * scale_att
        )
        grad_keys = (
            grad_keys
            + jnp.einsum(
                "shqk,shqe->shke", grad_scores, query_block, preferred_element_type=jnp.float32
            )
            * scale_att
        )
        grad_values = grad_values + jnp.einsum(
            "shqk,shqe->shke",
            attention.astype(jnp.bfloat16),
            grad_block,
            preferred_element_type=jnp.float32,
        )
    return (jnp.concatenate(grad_blocks, axis=2), grad_keys, grad_values)


def update_step(gradient_term, moment, weight_matrix, average, learning_rate):
    updated_moment = MOMENTUM_FACTOR * moment + gradient_term
    updated_weight = weight_matrix * (
        1.0 - learning_rate * WEIGHT_DECAY * ADAPTER_SCALE
    ) - learning_rate * (gradient_term + MOMENTUM_FACTOR * updated_moment)
    new_average = AVERAGE_KEEP * average + (1.0 - AVERAGE_KEEP) * updated_weight
    return (updated_moment, updated_weight, new_average)


def local(
    inputs,
    cotangent,
    groups,
    counts,
    vector_parameters,
    query_value_bias,
    hidden_bias,
    query_key_value_weight,
    attention_output_weight,
    hidden_weight,
    hidden_output_weight,
    adapter_down,
    adapter_up,
    momentum_down,
    momentum_up,
    average_down,
    average_up,
):
    seq_count, length, width_value = inputs.shape
    row_count = seq_count * length
    resid_in = inputs.reshape(row_count, width_value).astype(jnp.float32)
    first_norm_output = layer_norm(resid_in, vector_parameters[0], vector_parameters[1]).astype(
        jnp.bfloat16
    )
    local_width = query_key_value_weight.shape[2]
    column_start = lax.axis_index("tensor") * local_width
    down_reduced = adapter_down.astype(jnp.bfloat16)
    up_reduced = adapter_up.astype(jnp.bfloat16)
    up_local = lax.dynamic_slice_in_dim(up_reduced, column_start, local_width, 2)
    projected_rows = jnp.einsum(
        "rd,cde->cre", first_norm_output, query_key_value_weight, preferred_element_type=jnp.float32
    )
    adapter_input = jnp.einsum(
        "wo,qob->qwb", first_norm_output, down_reduced, preferred_element_type=jnp.float32
    ).astype(jnp.bfloat16)
    adapter_output = jnp.einsum(
        "iga,iaj->igj", adapter_input, up_local, preferred_element_type=jnp.float32
    )
    query_rows = (
        projected_rows[0] + query_value_bias[0] + ADAPTER_SCALE * adapter_output[0]
    ).astype(jnp.bfloat16)
    keys_low = projected_rows[1].astype(jnp.bfloat16)
    value_reduced = (
        projected_rows[2] + query_value_bias[1] + ADAPTER_SCALE * adapter_output[1]
    ).astype(jnp.bfloat16)
    scale_att = HEAD ** (-0.5)
    query_heads = to_heads(query_rows, seq_count, length)
    key_heads = to_heads(keys_low, seq_count, length)
    value_heads = to_heads(value_reduced, seq_count, length)
    heads_out, log_totals = attend(query_heads, key_heads, value_heads, scale_att)
    merged = to_rows(heads_out).astype(jnp.bfloat16)
    attn_part = jnp.dot(merged, attention_output_weight, preferred_element_type=jnp.float32)
    tile = row_count // lax.axis_size("tensor")
    row_offset = lax.axis_index("tensor") * tile
    one_hot = groups[:, None] == jnp.arange(counts.shape[0])[None, :]
    seq_counts = jnp.sum(jnp.where(one_hot, counts[None, :], 0), axis=1).astype(jnp.float32)
    seq_weight = COUNT_BASE / seq_counts
    grad_out = (cotangent.astype(jnp.float32) * seq_weight[:, None, None]).reshape(
        row_count, width_value
    )
    grad_low = grad_out.astype(jnp.bfloat16)
    attn_share = lax.psum_scatter(
        attn_part.astype(jnp.bfloat16), "tensor", scatter_dimension=0, tiled=True
    ).astype(jnp.float32)
    input_share = lax.dynamic_slice_in_dim(resid_in, row_offset, tile, 0)
    resid_share = input_share + attn_share + vector_parameters[4]
    norm_share = layer_norm(resid_share, vector_parameters[2], vector_parameters[3]).astype(
        jnp.bfloat16
    )
    norm2 = lax.all_gather(norm_share, "tensor", axis=0, tiled=True)
    preact = jnp.dot(norm2, hidden_weight, preferred_element_type=jnp.float32) + hidden_bias
    act_low = jax.nn.gelu(preact, approximate=True).astype(jnp.bfloat16)
    preact, mlp_part = (
        preact,
        jnp.dot(act_low, hidden_output_weight, preferred_element_type=jnp.float32),
    )
    mlp_share = lax.psum_scatter(
        mlp_part.astype(jnp.bfloat16), "tensor", scatter_dimension=0, tiled=True
    ).astype(jnp.float32)
    output_share = (resid_share + mlp_share + vector_parameters[5]).astype(jnp.bfloat16)
    output_rows = lax.all_gather(output_share, "tensor", axis=0, tiled=True)
    grad_act = jnp.einsum(
        "rd,fd->rf", grad_low, hidden_output_weight, preferred_element_type=jnp.float32
    )
    grad_pre = gelu_back(preact, grad_act).astype(jnp.bfloat16)
    grad_norm_share = lax.psum_scatter(
        jnp.einsum("rf,df->rd", grad_pre, hidden_weight, preferred_element_type=jnp.float32).astype(
            jnp.bfloat16
        ),
        "tensor",
        scatter_dimension=0,
        tiled=True,
    ).astype(jnp.float32)
    grad_out_share = lax.dynamic_slice_in_dim(grad_out, row_offset, tile, 0)
    grad_resid_share = grad_out_share + norm_back(
        resid_share, vector_parameters[2], vector_parameters[3], grad_norm_share
    )
    grad_resid_low = lax.all_gather(
        grad_resid_share.astype(jnp.bfloat16), "tensor", axis=0, tiled=True
    )
    grad_merged = jnp.einsum(
        "rd,ed->re", grad_resid_low, attention_output_weight, preferred_element_type=jnp.float32
    ).astype(jnp.bfloat16)
    grad_q, grad_k, grad_v = attend_back(
        query_heads,
        key_heads,
        value_heads,
        log_totals,
        to_heads(grad_merged, seq_count, length),
        scale_att,
    )
    grad_qkv = jnp.stack([to_rows(grad_q), to_rows(grad_k), to_rows(grad_v)]).astype(jnp.bfloat16)
    grad_norm1 = jnp.einsum(
        "cre,cde->rd", grad_qkv, query_key_value_weight, preferred_element_type=jnp.float32
    )
    query_value_gradient = jnp.stack([grad_qkv[0], grad_qkv[2]])
    adapter_input_gradient = ADAPTER_SCALE * jnp.einsum(
        "cre,cke->crk", query_value_gradient, up_local, preferred_element_type=jnp.float32
    )
    grad_norm1 = grad_norm1 + jnp.einsum(
        "ibp,inp->bn",
        adapter_input_gradient,
        down_reduced.astype(jnp.float32),
        precision=lax.Precision.HIGHEST,
    )
    grad_a_part = jnp.einsum(
        "rd,crk->cdk",
        first_norm_output,
        adapter_input_gradient,
        precision=lax.Precision.HIGHEST,
        preferred_element_type=jnp.float32,
    )
    local_up_gradient = ADAPTER_SCALE * jnp.einsum(
        "ipg,ipd->igd", adapter_input, query_value_gradient, preferred_element_type=jnp.float32
    )
    grad_b_part = lax.dynamic_update_slice(
        jnp.zeros((2, adapter_up.shape[1], width_value), jnp.float32),
        local_up_gradient,
        (0, 0, column_start),
    )
    grad_norm1_share = lax.psum_scatter(
        grad_norm1.astype(jnp.bfloat16), "tensor", scatter_dimension=0, tiled=True
    ).astype(jnp.float32)
    grad_input_share = grad_resid_share + norm_back(
        input_share, vector_parameters[0], vector_parameters[1], grad_norm1_share
    )
    grad_a_sum, grad_b_sum, weight_sum = lax.psum(
        (grad_a_part, grad_b_part, jnp.sum(seq_weight)), ("dp", "tensor")
    )
    mean_weight = weight_sum / (lax.axis_size("dp") * lax.axis_size("tensor") * seq_count)
    tokens_all = lax.axis_size("dp") * seq_count * length
    input_grad = lax.all_gather(
        (grad_input_share / mean_weight).astype(jnp.bfloat16), "tensor", axis=0, tiled=True
    )
    down_gradient = grad_a_sum / (mean_weight * tokens_all)
    up_gradient = grad_b_sum / (mean_weight * tokens_all)
    learning_rate = RATE_BASE * math.sqrt(tokens_all)
    updated_momentum_down, updated_down, updated_average_down = update_step(
        down_gradient, momentum_down, adapter_down, average_down, learning_rate
    )
    updated_momentum_up, updated_up, updated_average_up = update_step(
        up_gradient, momentum_up, adapter_up, average_up, learning_rate
    )
    block_out = output_rows.reshape(seq_count, length, width_value)
    input_grad = input_grad.reshape(seq_count, length, width_value)
    return (
        block_out,
        input_grad,
        down_gradient,
        up_gradient,
        updated_momentum_down,
        updated_momentum_up,
        updated_down,
        updated_up,
        updated_average_down,
        updated_average_up,
        updated_down.astype(jnp.bfloat16),
        updated_up.astype(jnp.bfloat16),
    )


QUARTER = 256
LANES = 128
BIAS_ROWS = 16
F32 = jnp.float32
BF16 = jnp.bfloat16
NT = (((1,), (1,)), ((), ()))


def dot(a, b):
    return lax.dot_general(a, b, (((1,), (0,)), ((), ())), preferred_element_type=F32)


def dot_nt(a, b):
    return lax.dot_general(a, b, NT, preferred_element_type=F32)


def parity(t):
    return (t ^ (t >> 1)) & 1


def tok_block(t):
    return parity(t) * 2 + ((t >> 1) & 1)


def rows_stats(rows):
    mean = jnp.mean(rows, axis=-1, keepdims=True)
    center = rows - mean
    rstd = lax.rsqrt(jnp.mean(center * center, axis=-1, keepdims=True) + NORM_EPS)
    return center * rstd, rstd


def norm_grad(xhat, rstd, gain, upstream):
    e = upstream * gain
    inner = jnp.mean(e * xhat, axis=-1, keepdims=True)
    return rstd * (e - jnp.mean(e, axis=-1, keepdims=True) - xhat * inner)


def seq_weight_of(groups_ref, counts_ref):
    count = counts_ref[groups_ref[0]]
    return COUNT_BASE / jnp.full((1, LANES), count, jnp.int32).astype(F32)


def cost(flops, nbytes, trans=0):
    return pl.CostEstimate(flops=int(flops), bytes_accessed=int(nbytes), transcendentals=int(trans))


def whole(shape):
    return pl.BlockSpec(shape, lambda *a: (0,) * len(shape))


def smem():
    return pl.BlockSpec(memory_space=pltpu.SMEM)


def call(
    kernel, grid, in_specs, out_specs, out_shape, args, prefetch, scratch=(), est=None, vmem=48
):
    return pl.pallas_call(
        kernel,
        grid_spec=pltpu.PrefetchScalarGridSpec(
            num_scalar_prefetch=len(prefetch),
            grid=grid,
            in_specs=in_specs,
            out_specs=out_specs,
            scratch_shapes=list(scratch),
        ),
        out_shape=out_shape,
        cost_estimate=est,
        compiler_params=pltpu.CompilerParams(vmem_limit_bytes=vmem * 1024 * 1024),
    )(*prefetch, *args)


def sds(shape, dtype):
    return jax.ShapeDtypeStruct(shape, dtype)


def fill_pack(out_ref, wh_ref, wo_ref, hb_ref):
    width = wh_ref.shape[0]
    out_ref[0, 0:width, :] = wh_ref[...]
    for j in range(width // QUARTER):
        out_ref[0, width + QUARTER * j : width + QUARTER * (j + 1), :] = wo_ref[
            :, QUARTER * j : QUARTER * (j + 1)
        ]
    bias = hb_ref[...]
    high = bias.astype(BF16)
    rest = bias - high.astype(F32)
    mid = rest.astype(BF16)
    low = (rest - mid.astype(F32)).astype(BF16)
    row = lax.broadcasted_iota(jnp.int32, (BIAS_ROWS, QUARTER), 0)
    spread = lambda v: jnp.broadcast_to(v.astype(F32), (BIAS_ROWS, QUARTER))
    packed = jnp.where(row == 0, spread(high), jnp.where(row == 1, spread(mid), spread(low)))
    out_ref[0, 2 * width : 2 * width + BIAS_ROWS, :] = jnp.where(row < 3, packed, 0.0).astype(BF16)


def pack_kernel(which_ref, wh_ref, wo_ref, hb_ref, out_ref):
    fill_pack(out_ref, wh_ref, wo_ref, hb_ref)


def fetch_kernel(core_ref, whx, wox, hbx, why, woy, hby, proj_ref, x_ref, y_ref, d_ref):
    width = whx.shape[0]
    half = proj_ref.shape[0]
    for ref, ops in ((x_ref, (whx, wox, hbx)), (y_ref, (why, woy, hby))):
        fill_pack(ref, *ops)
        for j in range(width // QUARTER):
            base = 2 * width + BIAS_ROWS + half * j
            ref[0, base : base + half, :] = proj_ref[:, QUARTER * j : QUARTER * (j + 1)]
    d_ref[...] = proj_ref[...]


def fetch_packs(core, hidden_weight, hidden_output_weight, hidden_bias, projection):
    width = hidden_weight.shape[0]
    half = projection.shape[0] // 2
    rows = 2 * width + BIAS_ROWS + half * (width // QUARTER)
    bias = hidden_bias.reshape(1, -1)
    triple = (hidden_weight, hidden_output_weight, bias)
    specs = []
    for base in (0, 2):
        specs += [
            pl.BlockSpec((width, QUARTER), lambda i, c, base=base: (0, base + c[0])),
            pl.BlockSpec((QUARTER, width), lambda i, c, base=base: (base + c[0], 0)),
            pl.BlockSpec((1, QUARTER), lambda i, c, base=base: (0, base + c[0])),
        ]
    return call(
        fetch_kernel,
        (1,),
        specs + [pl.BlockSpec((half, width), lambda i, c: (c[0], 0))],
        [whole((1, rows, QUARTER)), whole((1, rows, QUARTER)), whole((half, width))],
        [sds((1, rows, QUARTER), BF16)] * 2 + [sds((half, width), BF16)],
        (*triple, *triple, projection),
        (core,),
        est=cost(0, 8 * rows * QUARTER),
        vmem=62,
    )


def pack(which, count, hidden_weight, hidden_output_weight, hidden_bias):
    width = hidden_weight.shape[0]
    rows = 2 * width + BIAS_ROWS
    return call(
        pack_kernel,
        (count,),
        [
            pl.BlockSpec((width, QUARTER), lambda i, w: (0, w[i])),
            pl.BlockSpec((QUARTER, width), lambda i, w: (w[i], 0)),
            pl.BlockSpec((1, QUARTER), lambda i, w: (0, w[i])),
        ],
        pl.BlockSpec((1, rows, QUARTER), lambda i, w: (i, 0, 0)),
        sds((count, rows, QUARTER), BF16),
        (hidden_weight, hidden_output_weight, hidden_bias.reshape(1, -1)),
        (which,),
        est=cost(0, 4 * rows * QUARTER * count),
    )


def qkv_kernel(
    meta_ref, x_ref, vec_ref, w_ref, qvb_ref, down_ref, up_ref,
    q_ref, k_ref, v_ref, n_ref, lora_ref, down_s, up_s,
):
    rank = down_ref.shape[1]
    cols = w_ref.shape[2]

    @pl.when(pl.program_id(0) == 0)
    def _():
        down_s[...] = jnp.zeros_like(down_s)
        up_s[...] = jnp.zeros_like(up_s)
        down_s[0 : 2 * rank, :] = jnp.concatenate([down_ref[0], down_ref[1]], axis=0)
        up_s[0:rank, 0:cols] = up_ref[0]
        up_s[rank : 2 * rank, cols : 2 * cols] = up_ref[1]

    xhat, _ = rows_stats(x_ref[0].astype(F32))
    norm1 = (xhat * vec_ref[0:1, :] + vec_ref[1:2, :]).astype(BF16)
    n_ref[...] = norm1
    lora = dot_nt(norm1, down_s[...].astype(BF16)).astype(BF16)
    lora_ref[...] = lora
    adapt = ADAPTER_SCALE * dot(lora, up_s[...].astype(BF16))
    q = dot(norm1, w_ref[0]) + qvb_ref[0:1, :] + adapt[:, 0:cols]
    q_ref[...] = q.astype(BF16)
    k_ref[...] = dot(norm1, w_ref[1]).astype(BF16)
    v = dot(norm1, w_ref[2]) + qvb_ref[1:2, :] + adapt[:, cols : 2 * cols]
    v_ref[...] = v.astype(BF16)


def qkv(meta, x, vec, w, qvb, down_t, up):
    length, width = x.shape[1:]
    cols = w.shape[2]
    rank = up.shape[1]
    block = pl.BlockSpec((QUARTER, cols), lambda i, m: (i, 0))
    return call(
        qkv_kernel,
        (length // QUARTER,),
        [
            pl.BlockSpec((1, QUARTER, width), lambda i, m: (0, i, 0)),
            whole(vec.shape),
            whole(w.shape),
            whole(qvb.shape),
            whole(down_t.shape),
            pl.BlockSpec((2, rank, cols), lambda i, m: (0, 0, m[0] & 3)),
        ],
        [
            block,
            block,
            block,
            pl.BlockSpec((QUARTER, width), lambda i, m: (i, 0)),
            pl.BlockSpec((QUARTER, LANES), lambda i, m: (i, 0)),
        ],
        [
            sds((length, cols), BF16),
            sds((length, cols), BF16),
            sds((length, cols), BF16),
            sds((length, width), BF16),
            sds((length, LANES), BF16),
        ],
        (x, vec, w, qvb, down_t, up),
        (meta,),
        scratch=[pltpu.VMEM((LANES, width), F32), pltpu.VMEM((LANES, 2 * cols), F32)],
        est=cost(2 * length * width * 3 * cols, 4 * length * width + 6 * width * cols + 6 * length * cols),
    )


def head_lanes(value, head):
    lane = lax.broadcasted_iota(jnp.int32, value.shape, 1)
    return jnp.where(lane // HEAD == head, value, jnp.zeros_like(value))


def attend_kernel(meta_ref, q_ref, k_ref, v_ref, p_ref, ot_ref, same_ref, other_ref, vt_s, o_s):
    length = q_ref.shape[0]
    half = length // 2
    vt_s[...] = v_ref[...].astype(F32).T.astype(BF16)
    below = lax.broadcasted_iota(jnp.int32, (QUARTER, QUARTER), 0) <= lax.broadcasted_iota(
        jnp.int32, (QUARTER, QUARTER), 1
    )

    @pl.loop(0, 2)
    def _(head):
        rows = pl.ds(pl.multiple_of(head * HEAD, HEAD), HEAD)
        for j in range(length // QUARTER):
            at = slice(QUARTER * j, QUARTER * (j + 1))
            seen = QUARTER * (j + 1)
            query = head_lanes(q_ref[at, :], head) * jnp.asarray(HEAD ** (-0.5), BF16)
            scores = dot_nt(k_ref[0:seen, :], query)
            last = jnp.where(below, scores[QUARTER * j :, :], MASK_FILL)
            scores = last if j == 0 else jnp.concatenate([scores[: QUARTER * j, :], last], axis=0)
            top = jnp.max(scores, axis=0, keepdims=True)
            exponent = jnp.exp(scores - top)
            inverse = 1.0 / jnp.sum(exponent, axis=0, keepdims=True)
            probs = (exponent * inverse).astype(BF16)
            p_ref[head, 0:seen, at] = probs
            ot_ref[rows, at] = dot(vt_s[rows, 0:seen], probs)

    o_s[...] = ot_ref[...].T.astype(BF16)
    start = pl.multiple_of(parity(meta_ref[0] & 3) * half, half)
    same_ref[...] = o_s[pl.ds(start, half), :]
    other_ref[...] = o_s[pl.ds(pl.multiple_of(half - start, half), half), :]


def attend_fast(meta, q, k, v):
    length, cols = q.shape
    pairs = cols // LANES
    block = pl.BlockSpec((length, LANES), lambda g, m: (0, g))
    half = pl.BlockSpec((length // 2, LANES), lambda g, m: (0, g))
    return call(
        attend_kernel,
        (pairs,),
        [block, block, block],
        [
            pl.BlockSpec((2, length, length), lambda g, m: (g, 0, 0)),
            pl.BlockSpec((LANES, length), lambda g, m: (g, 0)),
            half,
            half,
        ],
        [
            sds((2 * pairs, length, length), BF16),
            sds((cols, length), F32),
            sds((length // 2, cols), BF16),
            sds((length // 2, cols), BF16),
        ],
        (q, k, v),
        (meta,),
        scratch=[pltpu.VMEM((LANES, length), BF16), pltpu.VMEM((length, LANES), BF16)],
        est=cost(8 * length * length * cols, 4 * length * length * pairs + 10 * length * cols),
    )


def attend_back_kernel(
    meta_ref, q_ref, k_ref, v_ref, p_ref, ot_ref, go_ref, gx_ref, gy_ref, gd_ref,
    dq_ref, dk_ref, dv_ref, g_s, gt_s, kt_s, dqt_s, dk_s, dv_s,
):
    length = q_ref.shape[0]
    t = meta_ref[0] & 3
    for piece, who in ((go_ref, t), (gx_ref, t ^ 1), (gy_ref, t ^ 2), (gd_ref, t ^ 3)):
        start = pl.multiple_of(tok_block(who) * QUARTER, QUARTER)
        g_s[pl.ds(start, QUARTER), :] = piece[...]
    gt_s[...] = g_s[...].astype(F32).T
    kt_s[...] = k_ref[...].astype(F32).T.astype(BF16)
    dk_s[...] = jnp.zeros_like(dk_s)
    dv_s[...] = jnp.zeros_like(dv_s)
    scale = jnp.asarray(HEAD ** (-0.5), BF16)

    @pl.loop(0, 2)
    def _(head):
        rows = pl.ds(pl.multiple_of(head * HEAD, HEAD), HEAD)
        for j in range(length // QUARTER):
            at = slice(QUARTER * j, QUARTER * (j + 1))
            seen = QUARTER * (j + 1)
            query = head_lanes(q_ref[at, :], head) * scale
            grad = head_lanes(g_s[at, :], head)
            inner = jnp.sum(gt_s[rows, at] * ot_ref[rows, at], axis=0, keepdims=True)
            probs = p_ref[head, 0:seen, at]
            grad_probs = dot_nt(v_ref[0:seen, :], grad)
            grad_scores = (probs.astype(F32) * (grad_probs - inner)).astype(BF16)
            dv_s[0:seen, :] += dot(probs, grad)
            dk_s[0:seen, :] += dot(grad_scores, query)
            dqt_s[rows, at] = dot(kt_s[rows, 0:seen], grad_scores)

    dq_ref[...] = (dqt_s[...].T * (HEAD ** (-0.5))).astype(BF16)
    dk_ref[...] = dk_s[...].astype(BF16)
    dv_ref[...] = dv_s[...].astype(BF16)


def attend_back_fast(meta, q, k, v, probs, out_t, pieces):
    length, cols = q.shape
    pairs = cols // LANES
    block = pl.BlockSpec((length, LANES), lambda g, m: (0, g))
    piece = pl.BlockSpec((QUARTER, LANES), lambda g, m: (0, g))
    return call(
        attend_back_kernel,
        (pairs,),
        [
            block,
            block,
            block,
            pl.BlockSpec((2, length, length), lambda g, m: (g, 0, 0)),
            pl.BlockSpec((LANES, length), lambda g, m: (g, 0)),
            piece,
            piece,
            piece,
            piece,
        ],
        [block, block, block],
        [sds((length, cols), BF16)] * 3,
        (q, k, v, probs, out_t, *pieces),
        (meta,),
        scratch=[
            pltpu.VMEM((length, LANES), BF16),
            pltpu.VMEM((LANES, length), F32),
            pltpu.VMEM((LANES, length), BF16),
            pltpu.VMEM((LANES, length), F32),
            pltpu.VMEM((length, LANES), F32),
            pltpu.VMEM((length, LANES), F32),
        ],
        est=cost(16 * length * length * cols, 4 * length * length * pairs + 16 * length * cols),
    )


def mlp_kernel(
    meta_ref, groups_ref, counts_ref, x_ref, cot_ref, vec_ref,
    ho_ref, hx_ref, hy_ref, hd_ref, wof_ref,
    own_ref, xa_ref, xb_ref, ya_ref, yb_ref,
    gn_ref, mlp_ref, resid_ref, n2_s, low_s, h_s, gn_s, mlp_s, buf, sem,
):
    width = x_ref.shape[2]
    blocks = own_ref.shape[0]
    total = blocks + 4
    extras = (xa_ref, xb_ref, ya_ref, yb_ref)
    depth = own_ref.shape[1]

    def fetch(i, slot):
        @pl.when(i < blocks)
        def _():
            pltpu.make_async_copy(own_ref.at[jnp.minimum(i, blocks - 1)], buf.at[slot], sem.at[slot]).start()

        for n, ref in enumerate(extras):
            @pl.when(i == blocks + n)
            def _(ref=ref):
                pltpu.make_async_copy(ref.at[0, 0:depth], buf.at[slot], sem.at[slot]).start()

    fetch(0, 0)
    local = ho_ref.shape[1]
    for n, ref in enumerate((ho_ref, hx_ref, hy_ref, hd_ref)):
        h_s[:, local * n : local * (n + 1)] = ref[...]
    resid = x_ref[0].astype(F32) + dot(h_s[...], wof_ref[...]) + vec_ref[4:5, :]
    resid_ref[...] = resid
    xhat, _ = rows_stats(resid)
    n2_s[...] = (xhat * vec_ref[2:3, :] + vec_ref[3:4, :]).astype(BF16)
    weight = seq_weight_of(groups_ref, counts_ref)[:, 0:1]
    low_s[...] = (cot_ref[0].astype(F32) * weight).astype(BF16)
    gn_s[...] = jnp.zeros_like(gn_s)
    mlp_s[...] = jnp.zeros_like(mlp_s)

    @pl.loop(0, total)
    def _(i):
        slot = i & 1
        pltpu.make_async_copy(own_ref.at[0], buf.at[slot], sem.at[slot]).wait()

        @pl.when(i + 1 < total)
        def _():
            fetch(i + 1, 1 - slot)

        wh = buf[slot, 0:width, :]
        tail = buf[slot, 2 * width : 2 * width + BIAS_ROWS, :].astype(F32)
        bias = tail[0:1, :] + tail[1:2, :] + tail[2:3, :]
        pre = dot(n2_s[...], wh) + bias
        grad_act = jnp.zeros_like(pre)
        for j in range(width // QUARTER):
            piece = buf[slot, width + QUARTER * j : width + QUARTER * (j + 1), :]
            grad_act = grad_act + dot_nt(low_s[:, QUARTER * j : QUARTER * (j + 1)], piece)
        root = math.sqrt(2.0 / math.pi)
        square = pre * pre
        turn = jnp.tanh(root * (pre + 0.044715 * (square * pre)))
        act = (0.5 * pre * (1.0 + turn)).astype(BF16)
        slope = 0.5 * (1.0 + turn) + 0.5 * pre * (1.0 - turn * turn) * (
            root * (1.0 + 3.0 * 0.044715 * square)
        )
        grad_pre = (grad_act * slope).astype(BF16)
        gn_s[...] += dot_nt(grad_pre, wh)
        for j in range(width // QUARTER):
            piece = buf[slot, width + QUARTER * j : width + QUARTER * (j + 1), :]
            mlp_s[:, QUARTER * j : QUARTER * (j + 1)] += dot(act, piece)

    gn_ref[...] = gn_s[...].astype(gn_ref.dtype)
    mlp_ref[...] = mlp_s[...].astype(mlp_ref.dtype)


def mlp_fast(final, meta, groups, counts, x, cot, vec, heads, wof, packs):
    width = x.shape[2]
    local = heads[0].shape[1]
    kind = F32 if final else BF16
    flip = 0 if final else 3
    rows = pl.BlockSpec((1, QUARTER, width), lambda i, m: (0, tok_block((m[0] & 3) ^ flip), 0))
    head = pl.BlockSpec((QUARTER, local), lambda i, m: ((((m[0] & 3) ^ flip) >> 1) & 1, 0))
    any_ = pl.BlockSpec(memory_space=pl.ANY)
    out = whole((QUARTER, width))
    depth = 2 * width + BIAS_ROWS
    hidden = QUARTER * (packs[0].shape[0] + 4)
    return call(
        mlp_kernel,
        (1,),
        [smem(), smem(), rows, rows, whole(vec.shape), head, head, head, head, whole(wof.shape)]
        + [any_] * 5,
        [out, out, out],
        [sds((QUARTER, width), kind), sds((QUARTER, width), kind), sds((QUARTER, width), F32)],
        (groups, counts, x, cot, vec, *heads, wof, *packs),
        (meta,),
        scratch=[
            pltpu.VMEM((QUARTER, width), BF16),
            pltpu.VMEM((QUARTER, width), BF16),
            pltpu.VMEM((QUARTER, 4 * local), BF16),
            pltpu.VMEM((QUARTER, width), F32),
            pltpu.VMEM((QUARTER, width), F32),
            pltpu.VMEM((2, depth, QUARTER), BF16),
            pltpu.SemaphoreType.DMA((2,)),
        ],
        est=cost(
            8 * QUARTER * width * hidden + 2 * QUARTER * width * width,
            4 * width * hidden + 2 * width * width + 16 * QUARTER * width,
            QUARTER * hidden,
        ),
    )


def project_kernel(meta_ref, own_ref, x0, x1, y0, y1, d0, d1, wof_ref):
    core = (meta_ref[0] >> 2) & 1
    local, width = own_ref.shape
    half = local // 2
    wof_ref[0:local, :] = own_ref[...]
    for n, (first, second) in enumerate(((x0, x1), (y0, y1), (d0, d1))):
        for ref, at in ((first, core), (second, 1 - core)):
            start = pl.multiple_of(local * (n + 1) + at * half, half)
            if n == 2:
                wof_ref[pl.ds(start, half), :] = ref[...]
            else:
                for j in range(width // QUARTER):
                    wof_ref[pl.ds(start, half), QUARTER * j : QUARTER * (j + 1)] = ref[
                        0, BIAS_ROWS + half * j : BIAS_ROWS + half * (j + 1), :
                    ]


def project(meta, own, packs, halves):
    local, width = own.shape
    depth = packs[0].shape[1]
    size = depth - 2 * width
    tail = pl.BlockSpec((pl.Element(1), pl.Element(size), pl.Element(QUARTER)), lambda i, m: (0, 2 * width, 0))
    return call(
        project_kernel,
        (1,),
        [whole(own.shape)] + [tail] * 4 + [whole(h.shape) for h in halves],
        whole((4 * local, width)),
        sds((4 * local, width), BF16),
        (own, *packs, *halves),
        (meta,),
        est=cost(0, 16 * local * width),
    )


def resid_back_kernel(
    meta_ref, groups_ref, counts_ref, own_ref, recv_ref, resid_ref, cot_ref, vec_ref, wof_ref,
    gr_ref, o_ref, x_ref, y_ref, d_ref,
):
    weight = seq_weight_of(groups_ref, counts_ref)[:, 0:1]
    grad = own_ref[...] + recv_ref[...].astype(F32)
    xhat, rstd = rows_stats(resid_ref[...])
    total = cot_ref[0].astype(F32) * weight + norm_grad(xhat, rstd, vec_ref[2:3, :], grad)
    gr_ref[...] = total
    low = total.astype(BF16)
    local = wof_ref.shape[0] // 4
    for n, ref in enumerate((o_ref, x_ref, y_ref, d_ref)):
        ref[...] = dot_nt(low, wof_ref[local * n : local * (n + 1), :]).astype(BF16)


def resid_back(meta, groups, counts, own, recv, resid, cot, vec, wof):
    width = own.shape[1]
    local = wof.shape[0] // 4
    piece = whole((QUARTER, local))
    full = whole((QUARTER, width))
    return call(
        resid_back_kernel,
        (1,),
        [
            smem(),
            smem(),
            full,
            full,
            full,
            pl.BlockSpec((1, QUARTER, width), lambda i, m: (0, tok_block(m[0] & 3), 0)),
            whole(vec.shape),
            whole(wof.shape),
        ],
        [full, piece, piece, piece, piece],
        [sds((QUARTER, width), F32)] + [sds((QUARTER, local), BF16)] * 4,
        (groups, counts, own, recv, resid, cot, vec, wof),
        (meta,),
        est=cost(2 * QUARTER * width * width, 16 * QUARTER * width + 2 * width * width),
    )


def adapter_inner(dq, dv, up_s, cols):
    ups = up_s[...].astype(BF16)
    return ADAPTER_SCALE * (dot_nt(dq, ups[:, 0:cols]) + dot_nt(dv, ups[:, cols : 2 * cols]))


def fill_up(up_s, up_ref, cols):
    rank = up_ref.shape[1]
    up_s[...] = jnp.zeros_like(up_s)
    for copy in (0, 2):
        up_s[copy * rank : (copy + 1) * rank, 0:cols] = up_ref[0]
        up_s[(copy + 1) * rank : (copy + 2) * rank, cols : 2 * cols] = up_ref[1]


def split_inner(inner, rank):
    high = inner.astype(BF16)
    low = (inner - high.astype(F32)).astype(BF16)
    lane = lax.broadcasted_iota(jnp.int32, inner.shape, 1)
    return jnp.where(lane < 2 * rank, high.astype(F32), low.astype(F32))


def grads_kernel(
    meta_ref, groups_ref, counts_ref, dq_ref, dv_ref, up_ref, n_ref, lora_ref,
    grads_ref, up_s, dn_s, gu_s,
):
    i = pl.program_id(0)
    rank = up_ref.shape[1]
    cols = dq_ref.shape[1]

    @pl.when(i == 0)
    def _():
        fill_up(up_s, up_ref, cols)
        dn_s[...] = jnp.zeros_like(dn_s)
        gu_s[...] = jnp.zeros_like(gu_s)

    dq, dv = dq_ref[...], dv_ref[...]
    split = split_inner(adapter_inner(dq, dv, up_s, cols), rank)
    dn_s[...] += dot(split.T.astype(BF16), n_ref[...])
    lt = lora_ref[...].astype(F32).T.astype(BF16)
    gu_s[...] += ADAPTER_SCALE * dot(lt, jnp.concatenate([dq, dv], axis=1))

    @pl.when(i == pl.num_programs(0) - 1)
    def _():
        grads_ref[...] = jnp.zeros_like(grads_ref)
        grads_ref[0 : 2 * rank, :] = dn_s[0 : 2 * rank, :] + dn_s[2 * rank : 4 * rank, :]
        start = pl.multiple_of((meta_ref[0] & 3) * cols, cols)
        grads_ref[2 * rank : 3 * rank, pl.ds(start, cols)] = gu_s[0:rank, 0:cols]
        grads_ref[3 * rank : 4 * rank, pl.ds(start, cols)] = gu_s[rank : 2 * rank, cols : 2 * cols]
        weight = seq_weight_of(groups_ref, counts_ref)[:, 0:1]
        grads_ref[4 * rank : 4 * rank + 8, :] = jnp.broadcast_to(weight, (8, grads_ref.shape[1]))


def adapter_grads(meta, groups, counts, dq, dv, up, norm1, lora):
    length, cols = dq.shape
    width = norm1.shape[1]
    rank = up.shape[1]
    rows = 2 * QUARTER
    block = pl.BlockSpec((rows, cols), lambda i, m: (i, 0))
    lanes = pl.BlockSpec((rows, LANES), lambda i, m: (i, 0))
    return call(
        grads_kernel,
        (length // rows,),
        [
            smem(),
            smem(),
            block,
            block,
            pl.BlockSpec((2, rank, cols), lambda i, m: (0, 0, m[0] & 3)),
            pl.BlockSpec((rows, width), lambda i, m: (i, 0)),
            lanes,
        ],
        whole((4 * rank + 8, width)),
        sds((4 * rank + 8, width), F32),
        (groups, counts, dq, dv, up, norm1, lora),
        (meta,),
        scratch=[
            pltpu.VMEM((LANES, 2 * cols), F32),
            pltpu.VMEM((LANES, width), F32),
            pltpu.VMEM((LANES, 2 * cols), F32),
        ],
        est=cost(2 * length * width * LANES, 2 * length * width + 4 * length * cols),
    )


def input_back_kernel(
    meta_ref, dq_ref, dk_ref, dv_ref, w_ref, down_ref, up_ref,
    ox_ref, oy_ref, od_ref, own_ref, down_s, up_s,
):
    i = pl.program_id(0)
    rank = down_ref.shape[1]
    cols = dq_ref.shape[1]

    @pl.when(i == 0)
    def _():
        fill_up(up_s, up_ref, cols)
        down_s[...] = jnp.zeros_like(down_s)
        both = jnp.concatenate([down_ref[0], down_ref[1]], axis=0)
        down_s[0 : 2 * rank, :] = both
        down_s[2 * rank : 4 * rank, :] = both

    dq, dv = dq_ref[...], dv_ref[...]
    split = split_inner(adapter_inner(dq, dv, up_s, cols), rank)
    grad = (
        dot_nt(dq, w_ref[0])
        + dot_nt(dk_ref[...], w_ref[1])
        + dot_nt(dv, w_ref[2])
        + dot(split.astype(BF16), down_s[...].astype(BF16))
    )
    for n, ref in enumerate((ox_ref, oy_ref, od_ref, own_ref)):
        @pl.when(i == n)
        def _(ref=ref):
            ref[...] = grad.astype(ref.dtype)


def input_back(meta, dq, dk, dv, w, down_t, up):
    length, cols = dq.shape
    width = w.shape[1]
    rank = up.shape[1]

    def who(i, m):
        return tok_block((m[0] & 3) ^ jnp.where(i == 3, 0, i + 1))

    block = pl.BlockSpec((QUARTER, cols), lambda i, m: (who(i, m), 0))
    out = whole((QUARTER, width))
    return call(
        input_back_kernel,
        (4,),
        [
            block,
            block,
            block,
            whole(w.shape),
            whole(down_t.shape),
            pl.BlockSpec((2, rank, cols), lambda i, m: (0, 0, m[0] & 3)),
        ],
        [out, out, out, out],
        [sds((QUARTER, width), BF16)] * 3 + [sds((QUARTER, width), F32)],
        (dq, dk, dv, w, down_t, up),
        (meta,),
        scratch=[pltpu.VMEM((LANES, width), F32), pltpu.VMEM((LANES, 2 * cols), F32)],
        est=cost(6 * length * width * cols, 6 * width * cols + 6 * length * cols + 6 * length * width),
    )


def first_back_kernel(meta_ref, own_ref, a_ref, b_ref, c_ref, x_ref, gr_ref, vec_ref, out_ref):
    grad = own_ref[...] + a_ref[...].astype(F32) + b_ref[...].astype(F32) + c_ref[...].astype(F32)
    xhat, rstd = rows_stats(x_ref[0].astype(F32))
    out_ref[...] = (gr_ref[...] + norm_grad(xhat, rstd, vec_ref[0:1, :], grad)).astype(BF16)


def first_back(meta, own, pieces, x, grad_resid, vec):
    width = own.shape[1]
    full = whole((QUARTER, width))
    return call(
        first_back_kernel,
        (1,),
        [
            full,
            full,
            full,
            full,
            pl.BlockSpec((1, QUARTER, width), lambda i, m: (0, tok_block(m[0] & 3), 0)),
            full,
            whole(vec.shape),
        ],
        full,
        sds((QUARTER, width), BF16),
        (own, *pieces, x, grad_resid, vec),
        (meta,),
        est=cost(30 * QUARTER * width, 16 * QUARTER * width),
    )


def gather_kernel(scaled, meta_ref, *refs):
    out_ref = refs[-1]
    pieces = refs[:-1]
    if scaled:
        factor = scaled / refs[0][0:1, 0:1]
        pieces = refs[1:-1]
    i = pl.program_id(0)
    for n in range(4):
        parts = pieces[3:] if n == 3 else pieces[n : n + 1]

        @pl.when(i == n)
        def _(parts=parts):
            start = 0
            for ref in parts:
                rows = ref.shape[0]
                value = ref[...]
                if scaled:
                    value = (value.astype(F32) * factor).astype(BF16)
                out_ref[0, start : start + rows, :] = value
                start += rows


def gather_rows(meta, pieces, scaled=0.0, total=None):
    width = pieces[0].shape[1]
    extra = [total] if scaled else []
    specs = [pl.BlockSpec((8, width), lambda i, m: (total.shape[0] // 8 - 1, 0))] if scaled else []
    return call(
        functools.partial(gather_kernel, scaled),
        (4,),
        specs + [whole(p.shape) for p in pieces],
        pl.BlockSpec((1, QUARTER, width), lambda i, m: (0, tok_block((m[0] & 3) ^ i), 0)),
        sds((1, 4 * QUARTER, width), BF16),
        (*extra, *pieces),
        (meta,),
        est=cost(0, 16 * QUARTER * width),
    )


def update_kernel(tokens, devices, total_ref, d_ref, u_ref, md_ref, mu_ref, ad_ref, au_ref, *outs):
    gd_o, gu_o, md_o, mu_o, d_o, u_o, ad_o, au_o, cd_o, cu_o = outs
    rank = d_ref.shape[1]
    weight = total_ref[4 * rank : 4 * rank + 1, 0:1]
    mean_weight = weight / devices
    rate = RATE_BASE * math.sqrt(tokens)
    for c in range(2):
        for base, g_o, m_ref, m_o, w_ref, w_o, a_ref, a_o, c_o in (
            (0, gd_o, md_ref, md_o, d_ref, d_o, ad_ref, ad_o, cd_o),
            (2 * rank, gu_o, mu_ref, mu_o, u_ref, u_o, au_ref, au_o, cu_o),
        ):
            gradient = total_ref[base + c * rank : base + (c + 1) * rank, :] / (mean_weight * tokens)
            moment, new, average = update_step(gradient, m_ref[c], w_ref[c], a_ref[c], rate)
            g_o[c] = gradient
            m_o[c] = moment
            w_o[c] = new
            a_o[c] = average
            c_o[c] = new.astype(BF16)


def update(tokens, devices, total, down_t, up, mom_d, mom_u, avg_d, avg_u):
    shapes = [whole(total.shape)] + [whole(down_t.shape)] * 6
    kinds = [F32] * 8 + [BF16] * 2
    return call(
        functools.partial(update_kernel, float(tokens), float(devices)),
        (1,),
        shapes,
        [whole(down_t.shape)] * 10,
        [sds(down_t.shape, kind) for kind in kinds],
        (total, down_t, up, mom_d, mom_u, avg_d, avg_u),
        (),
        est=cost(0, 18 * 4 * down_t.size),
    )


def local_fast(
    dp_size,
    inputs,
    cotangent,
    groups,
    counts,
    vector_parameters,
    query_value_bias,
    hidden_bias,
    query_key_value_weight,
    attention_output_weight,
    hidden_weight,
    hidden_output_weight,
    adapter_down,
    adapter_up,
    momentum_down,
    momentum_up,
    average_down,
    average_up,
):
    axes = ("dp", "tensor")

    def send(value, dp_flip, t_flip):
        pairs = [
            (d * 4 + t, (d ^ dp_flip) * 4 + (t ^ t_flip)) for d in range(dp_size) for t in range(4)
        ]
        return lax.ppermute(value, axes, pairs)

    tensor_at = lax.axis_index("tensor")
    core = lax.axis_index("dp") & 1
    meta = (tensor_at + 4 * core).astype(jnp.int32).reshape(1)
    down_t = jnp.swapaxes(adapter_down, 1, 2)
    vec = vector_parameters
    length = inputs.shape[1]

    one = core.astype(jnp.int32).reshape(1)
    ffn = (hidden_weight, hidden_output_weight, hidden_bias)
    pack_x, pack_y, pack_d = fetch_packs(one, *ffn, attention_output_weight)
    got_x = send(pack_x, 0, 1)
    got_y = send(pack_y, 0, 2)
    got_d = send(pack_d, 0, 3)

    q, k, v, norm1, lora = qkv(
        meta, inputs, vec, query_key_value_weight, query_value_bias, down_t, adapter_up
    )
    probs, out_t, same, other = attend_fast(meta, q, k, v)
    heads = [same, send(other, 0, 1), send(other, 0, 2), send(same, 0, 3)]
    swap_x = send(got_x, 1, 0)
    swap_y = send(got_y, 1, 0)
    swap_d = send(got_d, 1, 0)
    own_packs = pack(jnp.arange(4, dtype=jnp.int32), 4, *ffn)
    wof = project(
        meta, attention_output_weight, (got_x, swap_x, got_y, swap_y), (got_d, swap_d)
    )
    packs = [own_packs, got_x, swap_x, got_y, swap_y]

    gn_pair, mlp_pair, _ = mlp_fast(
        False, meta, groups, counts, inputs, cotangent, vec, heads, wof, packs
    )
    gn_recv = send(gn_pair, 0, 3)
    mlp_recv = send(mlp_pair, 0, 3)
    gn_own, mlp_own, resid = mlp_fast(
        True, meta, groups, counts, inputs, cotangent, vec, heads, wof, packs
    )
    grad_resid, g_own, g_x, g_y, g_d = resid_back(
        meta, groups, counts, gn_own, gn_recv, resid, cotangent, vec, wof
    )
    pieces = [g_own, send(g_x, 0, 1), send(g_y, 0, 2), send(g_d, 0, 3)]
    out_own = (resid + mlp_own + mlp_recv.astype(F32) + vec[5]).astype(BF16)
    half = QUARTER // 2

    def spread(own):
        from_x = send(own, 0, 1)
        from_y = send(own, 0, 2)
        cut_x, cut_y = from_x[:half], from_y[half:]
        return [own, from_x, from_y, send(cut_x, 0, 2), send(cut_y, 0, 1)]

    out_all = spread(out_own)

    dq, dk, dv = attend_back_fast(meta, q, k, v, probs, out_t, pieces)
    gx, gy, gd, g1_own = input_back(
        meta, dq, dk, dv, query_key_value_weight, down_t, adapter_up
    )
    g1 = [send(gx, 0, 1), send(gy, 0, 2), send(gd, 0, 3)]
    total = adapter_grads(meta, groups, counts, dq, dv, adapter_up, norm1, lora)
    sum_x = send(total, 0, 1)
    sum_y = send(total, 0, 2)
    sum_d = send(total, 0, 3)
    total = (total + sum_x) + (sum_y + sum_d)
    step = 1
    while step < dp_size:
        got = send(total, step, 0)
        total = total + got
        step *= 2
    in_own = first_back(meta, g1_own, g1, inputs, grad_resid, vec)
    in_all = spread(in_own)
    block_out = gather_rows(meta, out_all)
    copies = dp_size * 4
    input_grad = gather_rows(meta, in_all, scaled=float(copies), total=total)
    results = update(
        dp_size * length,
        copies,
        total,
        down_t,
        adapter_up,
        jnp.swapaxes(momentum_down, 1, 2),
        momentum_up,
        jnp.swapaxes(average_down, 1, 2),
        average_up,
    )
    results = [
        jnp.swapaxes(value, 1, 2) if number % 2 == 0 else value
        for number, value in enumerate(results)
    ]
    return (block_out, input_grad, *results)


def solution(mesh):
    in_specs = (
        P("dp", None, None),
        P("dp", None, None),
        P("dp"),
        P(),
        P(),
        P(None, "tensor"),
        P("tensor"),
        P(None, None, "tensor"),
        P("tensor", None),
        P(None, "tensor"),
        P("tensor", None),
        P(),
        P(),
        P(),
        P(),
        P(),
        P(),
    )
    out_specs = (
        P("dp", None, None),
        P("dp", None, None),
        P(),
        P(),
        P(),
        P(),
        P(),
        P(),
        P(),
        P(),
        P(),
        P(),
    )
    dp_size = mesh.shape["dp"]
    small = mesh.shape["tensor"] == 4 and dp_size & (dp_size - 1) == 0 and dp_size > 1

    def body(*args):
        if small and args[0].shape[0] == 1 and args[0].shape[1] == 4 * QUARTER:
            return local_fast(dp_size, *args)
        return local(*args)

    return jax.shard_map(body, mesh=mesh, in_specs=in_specs, out_specs=out_specs, check_vma=False)
```

```python
import functools
import math

import jax
import jax.numpy as jnp
from jax import lax
from jax.experimental import pallas as pl
from jax.experimental.pallas import tpu as pltpu
from jax.sharding import PartitionSpec as P


HEAD = 64


NORM_EPS = 1e-05
ADAPTER_SCALE = 8.0
MASK_FILL = -1e30
MOMENTUM_FACTOR = 0.9
AVERAGE_KEEP = 0.8
RATE_BASE = 0.025
WEIGHT_DECAY = 0.005
COUNT_BASE = 256.0


def layer_norm(value_rows, norm_gain, norm_bias):
    center = value_rows - jnp.mean(value_rows, axis=-1, keepdims=True)
    spread = jnp.mean(center * center, axis=-1, keepdims=True)
    return center * lax.rsqrt(spread + NORM_EPS) * norm_gain + norm_bias


def norm_back(value_rows, norm_gain, norm_bias, upstream):

    def local_norm(operand):
        return layer_norm(operand, norm_gain, norm_bias)

    _, backward_map = jax.vjp(local_norm, value_rows)
    return backward_map(upstream)[0]


def gelu_back(preact, upstream):

    def activate(operand):
        return jax.nn.gelu(operand, approximate=True)

    _, backward_map = jax.vjp(activate, preact)
    return backward_map(upstream)[0]


def to_heads(matrix, seq_count, length):
    return matrix.reshape(seq_count, length, -1, HEAD).transpose(0, 2, 1, 3)


def to_rows(tensor4):
    return tensor4.transpose(0, 2, 1, 3).reshape(-1, tensor4.shape[1] * tensor4.shape[3])


def block_scores(query_block, keys, offset, scale_att):
    scores = (
        jnp.einsum("shqe,shke->shqk", query_block, keys, preferred_element_type=jnp.float32)
        * scale_att
    )
    query_pos = offset + jnp.arange(query_block.shape[2])
    key_pos = jnp.arange(keys.shape[2])
    return jnp.where(key_pos[None, :] <= query_pos[:, None], scores, MASK_FILL)


def attend(query_rows, keys, value_rows, scale_att):
    length = query_rows.shape[2]
    block_len = min(512, length)
    outputs = []
    log_totals = []
    for offset in range(0, length, block_len):
        query_block = query_rows[:, :, offset : offset + block_len]
        scores = block_scores(query_block, keys, offset, scale_att)
        largest = jnp.max(scores, axis=-1, keepdims=True)
        exponent = jnp.exp(scores - largest)
        summed = jnp.sum(exponent, axis=-1, keepdims=True)
        attention = exponent / summed
        log_totals.append(largest + jnp.log(summed))
        outputs.append(
            jnp.einsum(
                "shqk,shke->shqe",
                attention.astype(jnp.bfloat16),
                value_rows,
                preferred_element_type=jnp.float32,
            )
        )
    return (jnp.concatenate(outputs, axis=2), log_totals)


def attend_back(query_rows, keys, value_rows, log_totals, grad_heads, scale_att):
    length = query_rows.shape[2]
    block_len = min(512, length)
    grad_blocks = []
    grad_keys = jnp.zeros(keys.shape, jnp.float32)
    grad_values = jnp.zeros(value_rows.shape, jnp.float32)
    for number, offset in enumerate(range(0, length, block_len)):
        query_block = query_rows[:, :, offset : offset + block_len]
        grad_block = grad_heads[:, :, offset : offset + block_len]
        scores = block_scores(query_block, keys, offset, scale_att)
        attention = jnp.exp(scores - log_totals[number])
        grad_attn = jnp.einsum(
            "shqe,shke->shqk", grad_block, value_rows, preferred_element_type=jnp.float32
        )
        row_inner = jnp.sum(grad_attn * attention, axis=-1, keepdims=True)
        grad_scores = (attention * (grad_attn - row_inner)).astype(jnp.bfloat16)
        grad_blocks.append(
            jnp.einsum("shqk,shke->shqe", grad_scores, keys, preferred_element_type=jnp.float32)
            * scale_att
        )
        grad_keys = (
            grad_keys
            + jnp.einsum(
                "shqk,shqe->shke", grad_scores, query_block, preferred_element_type=jnp.float32
            )
            * scale_att
        )
        grad_values = grad_values + jnp.einsum(
            "shqk,shqe->shke",
            attention.astype(jnp.bfloat16),
            grad_block,
            preferred_element_type=jnp.float32,
        )
    return (jnp.concatenate(grad_blocks, axis=2), grad_keys, grad_values)


def update_step(gradient_term, moment, weight_matrix, average, learning_rate):
    updated_moment = MOMENTUM_FACTOR * moment + gradient_term
    updated_weight = weight_matrix * (
        1.0 - learning_rate * WEIGHT_DECAY * ADAPTER_SCALE
    ) - learning_rate * (gradient_term + MOMENTUM_FACTOR * updated_moment)
    new_average = AVERAGE_KEEP * average + (1.0 - AVERAGE_KEEP) * updated_weight
    return (updated_moment, updated_weight, new_average)


def local(
    inputs,
    cotangent,
    groups,
    counts,
    vector_parameters,
    query_value_bias,
    hidden_bias,
    query_key_value_weight,
    attention_output_weight,
    hidden_weight,
    hidden_output_weight,
    adapter_down,
    adapter_up,
    momentum_down,
    momentum_up,
    average_down,
    average_up,
):
    seq_count, length, width_value = inputs.shape
    row_count = seq_count * length
    resid_in = inputs.reshape(row_count, width_value).astype(jnp.float32)
    first_norm_output = layer_norm(resid_in, vector_parameters[0], vector_parameters[1]).astype(
        jnp.bfloat16
    )
    local_width = query_key_value_weight.shape[2]
    column_start = lax.axis_index("tensor") * local_width
    down_reduced = adapter_down.astype(jnp.bfloat16)
    up_reduced = adapter_up.astype(jnp.bfloat16)
    up_local = lax.dynamic_slice_in_dim(up_reduced, column_start, local_width, 2)
    projected_rows = jnp.einsum(
        "rd,cde->cre", first_norm_output, query_key_value_weight, preferred_element_type=jnp.float32
    )
    adapter_input = jnp.einsum(
        "wo,qob->qwb", first_norm_output, down_reduced, preferred_element_type=jnp.float32
    ).astype(jnp.bfloat16)
    adapter_output = jnp.einsum(
        "iga,iaj->igj", adapter_input, up_local, preferred_element_type=jnp.float32
    )
    query_rows = (
        projected_rows[0] + query_value_bias[0] + ADAPTER_SCALE * adapter_output[0]
    ).astype(jnp.bfloat16)
    keys_low = projected_rows[1].astype(jnp.bfloat16)
    value_reduced = (
        projected_rows[2] + query_value_bias[1] + ADAPTER_SCALE * adapter_output[1]
    ).astype(jnp.bfloat16)
    scale_att = HEAD ** (-0.5)
    query_heads = to_heads(query_rows, seq_count, length)
    key_heads = to_heads(keys_low, seq_count, length)
    value_heads = to_heads(value_reduced, seq_count, length)
    heads_out, log_totals = attend(query_heads, key_heads, value_heads, scale_att)
    merged = to_rows(heads_out).astype(jnp.bfloat16)
    attn_part = jnp.dot(merged, attention_output_weight, preferred_element_type=jnp.float32)
    tile = row_count // lax.axis_size("tensor")
    row_offset = lax.axis_index("tensor") * tile
    one_hot = groups[:, None] == jnp.arange(counts.shape[0])[None, :]
    seq_counts = jnp.sum(jnp.where(one_hot, counts[None, :], 0), axis=1).astype(jnp.float32)
    seq_weight = COUNT_BASE / seq_counts
    grad_out = (cotangent.astype(jnp.float32) * seq_weight[:, None, None]).reshape(
        row_count, width_value
    )
    grad_low = grad_out.astype(jnp.bfloat16)
    attn_share = lax.psum_scatter(
        attn_part.astype(jnp.bfloat16), "tensor", scatter_dimension=0, tiled=True
    ).astype(jnp.float32)
    input_share = lax.dynamic_slice_in_dim(resid_in, row_offset, tile, 0)
    resid_share = input_share + attn_share + vector_parameters[4]
    norm_share = layer_norm(resid_share, vector_parameters[2], vector_parameters[3]).astype(
        jnp.bfloat16
    )
    norm2 = lax.all_gather(norm_share, "tensor", axis=0, tiled=True)
    preact = jnp.dot(norm2, hidden_weight, preferred_element_type=jnp.float32) + hidden_bias
    act_low = jax.nn.gelu(preact, approximate=True).astype(jnp.bfloat16)
    preact, mlp_part = (
        preact,
        jnp.dot(act_low, hidden_output_weight, preferred_element_type=jnp.float32),
    )
    mlp_share = lax.psum_scatter(
        mlp_part.astype(jnp.bfloat16), "tensor", scatter_dimension=0, tiled=True
    ).astype(jnp.float32)
    output_share = (resid_share + mlp_share + vector_parameters[5]).astype(jnp.bfloat16)
    output_rows = lax.all_gather(output_share, "tensor", axis=0, tiled=True)
    grad_act = jnp.einsum(
        "rd,fd->rf", grad_low, hidden_output_weight, preferred_element_type=jnp.float32
    )
    grad_pre = gelu_back(preact, grad_act).astype(jnp.bfloat16)
    grad_norm_share = lax.psum_scatter(
        jnp.einsum("rf,df->rd", grad_pre, hidden_weight, preferred_element_type=jnp.float32).astype(
            jnp.bfloat16
        ),
        "tensor",
        scatter_dimension=0,
        tiled=True,
    ).astype(jnp.float32)
    grad_out_share = lax.dynamic_slice_in_dim(grad_out, row_offset, tile, 0)
    grad_resid_share = grad_out_share + norm_back(
        resid_share, vector_parameters[2], vector_parameters[3], grad_norm_share
    )
    grad_resid_low = lax.all_gather(
        grad_resid_share.astype(jnp.bfloat16), "tensor", axis=0, tiled=True
    )
    grad_merged = jnp.einsum(
        "rd,ed->re", grad_resid_low, attention_output_weight, preferred_element_type=jnp.float32
    ).astype(jnp.bfloat16)
    grad_q, grad_k, grad_v = attend_back(
        query_heads,
        key_heads,
        value_heads,
        log_totals,
        to_heads(grad_merged, seq_count, length),
        scale_att,
    )
    grad_qkv = jnp.stack([to_rows(grad_q), to_rows(grad_k), to_rows(grad_v)]).astype(jnp.bfloat16)
    grad_norm1 = jnp.einsum(
        "cre,cde->rd", grad_qkv, query_key_value_weight, preferred_element_type=jnp.float32
    )
    query_value_gradient = jnp.stack([grad_qkv[0], grad_qkv[2]])
    adapter_input_gradient = ADAPTER_SCALE * jnp.einsum(
        "cre,cke->crk", query_value_gradient, up_local, preferred_element_type=jnp.float32
    )
    grad_norm1 = grad_norm1 + jnp.einsum(
        "ibp,inp->bn",
        adapter_input_gradient,
        down_reduced.astype(jnp.float32),
        precision=lax.Precision.HIGHEST,
    )
    grad_a_part = jnp.einsum(
        "rd,crk->cdk",
        first_norm_output,
        adapter_input_gradient,
        precision=lax.Precision.HIGHEST,
        preferred_element_type=jnp.float32,
    )
    local_up_gradient = ADAPTER_SCALE * jnp.einsum(
        "ipg,ipd->igd", adapter_input, query_value_gradient, preferred_element_type=jnp.float32
    )
    grad_b_part = lax.dynamic_update_slice(
        jnp.zeros((2, adapter_up.shape[1], width_value), jnp.float32),
        local_up_gradient,
        (0, 0, column_start),
    )
    grad_norm1_share = lax.psum_scatter(
        grad_norm1.astype(jnp.bfloat16), "tensor", scatter_dimension=0, tiled=True
    ).astype(jnp.float32)
    grad_input_share = grad_resid_share + norm_back(
        input_share, vector_parameters[0], vector_parameters[1], grad_norm1_share
    )
    grad_a_sum, grad_b_sum, weight_sum = lax.psum(
        (grad_a_part, grad_b_part, jnp.sum(seq_weight)), ("dp", "tensor")
    )
    mean_weight = weight_sum / (lax.axis_size("dp") * lax.axis_size("tensor") * seq_count)
    tokens_all = lax.axis_size("dp") * seq_count * length
    input_grad = lax.all_gather(
        (grad_input_share / mean_weight).astype(jnp.bfloat16), "tensor", axis=0, tiled=True
    )
    down_gradient = grad_a_sum / (mean_weight * tokens_all)
    up_gradient = grad_b_sum / (mean_weight * tokens_all)
    learning_rate = RATE_BASE * math.sqrt(tokens_all)
    updated_momentum_down, updated_down, updated_average_down = update_step(
        down_gradient, momentum_down, adapter_down, average_down, learning_rate
    )
    updated_momentum_up, updated_up, updated_average_up = update_step(
        up_gradient, momentum_up, adapter_up, average_up, learning_rate
    )
    block_out = output_rows.reshape(seq_count, length, width_value)
    input_grad = input_grad.reshape(seq_count, length, width_value)
    return (
        block_out,
        input_grad,
        down_gradient,
        up_gradient,
        updated_momentum_down,
        updated_momentum_up,
        updated_down,
        updated_up,
        updated_average_down,
        updated_average_up,
        updated_down.astype(jnp.bfloat16),
        updated_up.astype(jnp.bfloat16),
    )


QUARTER = 256
LANES = 128
BIAS_ROWS = 16
F32 = jnp.float32
BF16 = jnp.bfloat16
NT = (((1,), (1,)), ((), ()))


def dot(a, b):
    return lax.dot_general(a, b, (((1,), (0,)), ((), ())), preferred_element_type=F32)


def dot_nt(a, b):
    return lax.dot_general(a, b, NT, preferred_element_type=F32)


def parity(t):
    return (t ^ (t >> 1)) & 1


def tok_block(t):
    return parity(t) * 2 + ((t >> 1) & 1)


def rows_stats(rows):
    mean = jnp.mean(rows, axis=-1, keepdims=True)
    center = rows - mean
    rstd = lax.rsqrt(jnp.mean(center * center, axis=-1, keepdims=True) + NORM_EPS)
    return center * rstd, rstd


def norm_grad(xhat, rstd, gain, upstream):
    e = upstream * gain
    inner = jnp.mean(e * xhat, axis=-1, keepdims=True)
    return rstd * (e - jnp.mean(e, axis=-1, keepdims=True) - xhat * inner)


def seq_weight_of(groups_ref, counts_ref):
    count = counts_ref[groups_ref[0]]
    return COUNT_BASE / jnp.full((1, LANES), count, jnp.int32).astype(F32)


def cost(flops, nbytes, trans=0):
    return pl.CostEstimate(flops=int(flops), bytes_accessed=int(nbytes), transcendentals=int(trans))


def whole(shape):
    return pl.BlockSpec(shape, lambda *a: (0,) * len(shape))


def smem():
    return pl.BlockSpec(memory_space=pltpu.SMEM)


def call(
    kernel, grid, in_specs, out_specs, out_shape, args, prefetch, scratch=(), est=None, vmem=20,
    alias=None,
):
    return pl.pallas_call(
        kernel,
        grid_spec=pltpu.PrefetchScalarGridSpec(
            num_scalar_prefetch=len(prefetch),
            grid=grid,
            in_specs=in_specs,
            out_specs=out_specs,
            scratch_shapes=list(scratch),
        ),
        out_shape=out_shape,
        cost_estimate=est,
        input_output_aliases=alias or {},
        compiler_params=pltpu.CompilerParams(vmem_limit_bytes=vmem * 1024 * 1024),
    )(*prefetch, *args)


def sds(shape, dtype):
    return jax.ShapeDtypeStruct(shape, dtype)


def bias_rows(bias):
    high = bias.astype(BF16)
    rest = bias - high.astype(F32)
    mid = rest.astype(BF16)
    low = (rest - mid.astype(F32)).astype(BF16)
    shape = (BIAS_ROWS, bias.shape[1])
    row = lax.broadcasted_iota(jnp.int32, shape, 0)
    spread = lambda v: jnp.broadcast_to(v.astype(F32), shape)
    packed = jnp.where(row == 0, spread(high), jnp.where(row == 1, spread(mid), spread(low)))
    return jnp.where(row < 3, packed, 0.0).astype(BF16)


def turned(block):
    return block.astype(F32).T.astype(BF16)


def pack_kernel(wh_ref, wo_ref, hb_ref, out_ref):
    units = wo_ref.shape[0]
    out_ref[0, 0:units, :] = turned(wh_ref[...])
    out_ref[0, units : 2 * units, :] = wo_ref[...]
    for n in range(units // LANES):
        base = 2 * units + BIAS_ROWS * n
        out_ref[0, base : base + BIAS_ROWS, 0:LANES] = bias_rows(
            hb_ref[:, LANES * n : LANES * (n + 1)]
        )


def pack(hidden_weight, hidden_output_weight, hidden_bias):
    width, hidden = hidden_weight.shape
    count = hidden // QUARTER
    rows = 2 * QUARTER + BIAS_ROWS * (QUARTER // LANES)
    return call(
        pack_kernel,
        (count,),
        [
            pl.BlockSpec((width, QUARTER), lambda i: (0, i)),
            pl.BlockSpec((QUARTER, width), lambda i: (i, 0)),
            pl.BlockSpec((1, QUARTER), lambda i: (0, i)),
        ],
        pl.BlockSpec((1, rows, width), lambda i: (i, 0, 0)),
        sds((count, rows, width), BF16),
        (hidden_weight, hidden_output_weight, hidden_bias.reshape(1, -1)),
        (),
        est=cost(0, 4 * rows * width * count),
    )


def fetch_kernel(core_ref, whx, wox, hbx, why, woy, hby, proj_ref, xa_ref, xb_ref, ya_ref, yb_ref):
    half = proj_ref.shape[0]
    for refs, wh, wo, hb in (((xa_ref, xb_ref), whx, wox, hbx), ((ya_ref, yb_ref), why, woy, hby)):
        for n, ref in enumerate(refs):
            at = slice(LANES * n, LANES * (n + 1))
            ref[0:LANES, :] = turned(wh[:, at])
            ref[LANES : 2 * LANES, :] = wo[at, :]
            ref[2 * LANES : 2 * LANES + BIAS_ROWS, 0:LANES] = bias_rows(hb[:, at])
        refs[0][2 * LANES + BIAS_ROWS : 2 * LANES + BIAS_ROWS + half, :] = proj_ref[...]


def fetch_packs(core, hidden_weight, hidden_output_weight, hidden_bias, projection):
    width = hidden_weight.shape[0]
    half = projection.shape[0] // 2
    rows = 2 * LANES + BIAS_ROWS
    triple = (hidden_weight, hidden_output_weight, hidden_bias.reshape(1, -1))
    specs = []
    for base in (0, 2):
        specs += [
            pl.BlockSpec((width, QUARTER), lambda i, c, base=base: (0, base + c[0])),
            pl.BlockSpec((QUARTER, width), lambda i, c, base=base: (base + c[0], 0)),
            pl.BlockSpec((1, QUARTER), lambda i, c, base=base: (0, base + c[0])),
        ]
    shapes = [(rows + half, width), (rows, width)] * 2
    return call(
        fetch_kernel,
        (1,),
        specs + [pl.BlockSpec((half, width), lambda i, c: (c[0], 0))],
        [whole(shape) for shape in shapes],
        [sds(shape, BF16) for shape in shapes],
        (*triple, *triple, projection),
        (core,),
        est=cost(0, 16 * rows * width),
        vmem=62,
    )


def qkv_kernel(
    meta_ref, x_ref, vec_ref, w_ref, qvb_ref, down_ref, up_ref,
    q_ref, k_ref, v_ref, n_ref, lora_ref, down_s, up_s,
):
    rank = down_ref.shape[1]
    cols = w_ref.shape[2]

    @pl.when(pl.program_id(0) == 0)
    def _():
        down_s[...] = jnp.zeros_like(down_s)
        up_s[...] = jnp.zeros_like(up_s)
        down_s[0 : 2 * rank, :] = jnp.concatenate([down_ref[0], down_ref[1]], axis=0)
        up_s[0:rank, 0:cols] = up_ref[0]
        up_s[rank : 2 * rank, cols : 2 * cols] = up_ref[1]

    xhat, _ = rows_stats(x_ref[0].astype(F32))
    norm1 = (xhat * vec_ref[0:1, :] + vec_ref[1:2, :]).astype(BF16)
    n_ref[...] = norm1
    lora = dot_nt(norm1, down_s[...].astype(BF16)).astype(BF16)
    lora_ref[...] = lora
    adapt = ADAPTER_SCALE * dot(lora, up_s[...].astype(BF16))
    q = dot(norm1, w_ref[0]) + qvb_ref[0:1, :] + adapt[:, 0:cols]
    q_ref[...] = q.astype(BF16)
    k_ref[...] = dot(norm1, w_ref[1]).astype(BF16)
    v = dot(norm1, w_ref[2]) + qvb_ref[1:2, :] + adapt[:, cols : 2 * cols]
    v_ref[...] = v.astype(BF16)


def qkv(meta, x, vec, w, qvb, down_t, up):
    length, width = x.shape[1:]
    cols = w.shape[2]
    rank = up.shape[1]
    block = pl.BlockSpec((QUARTER, cols), lambda i, m: (i, 0))
    return call(
        qkv_kernel,
        (length // QUARTER,),
        [
            pl.BlockSpec((1, QUARTER, width), lambda i, m: (0, i, 0)),
            whole(vec.shape),
            whole(w.shape),
            whole(qvb.shape),
            whole(down_t.shape),
            pl.BlockSpec((2, rank, cols), lambda i, m: (0, 0, m[0] & 3)),
        ],
        [
            block,
            block,
            block,
            pl.BlockSpec((QUARTER, width), lambda i, m: (i, 0)),
            pl.BlockSpec((QUARTER, LANES), lambda i, m: (i, 0)),
        ],
        [
            sds((length, cols), BF16),
            sds((length, cols), BF16),
            sds((length, cols), BF16),
            sds((length, width), BF16),
            sds((length, LANES), BF16),
        ],
        (x, vec, w, qvb, down_t, up),
        (meta,),
        scratch=[pltpu.VMEM((LANES, width), F32), pltpu.VMEM((LANES, 2 * cols), F32)],
        est=cost(2 * length * width * 3 * cols, 4 * length * width + 6 * width * cols + 6 * length * cols),
    )


def head_lanes(value, head):
    lane = lax.broadcasted_iota(jnp.int32, value.shape, 1)
    return jnp.where(lane // HEAD == head, value, jnp.zeros_like(value))


def attend_kernel(meta_ref, q_ref, k_ref, v_ref, p_ref, ot_ref, same_ref, other_ref, vt_s, o_s):
    length = q_ref.shape[0]
    half = length // 2
    vt_s[...] = v_ref[...].astype(F32).T.astype(BF16)
    below = lax.broadcasted_iota(jnp.int32, (QUARTER, QUARTER), 0) <= lax.broadcasted_iota(
        jnp.int32, (QUARTER, QUARTER), 1
    )

    @pl.loop(0, 2)
    def _(head):
        rows = pl.ds(pl.multiple_of(head * HEAD, HEAD), HEAD)
        for j in range(length // QUARTER):
            at = slice(QUARTER * j, QUARTER * (j + 1))
            seen = QUARTER * (j + 1)
            query = head_lanes(q_ref[at, :], head) * jnp.asarray(HEAD ** (-0.5), BF16)
            scores = dot_nt(k_ref[0:seen, :], query)
            last = jnp.where(below, scores[QUARTER * j :, :], MASK_FILL)
            scores = last if j == 0 else jnp.concatenate([scores[: QUARTER * j, :], last], axis=0)
            top = jnp.max(scores, axis=0, keepdims=True)
            exponent = jnp.exp(scores - top)
            inverse = 1.0 / jnp.sum(exponent, axis=0, keepdims=True)
            probs = (exponent * inverse).astype(BF16)
            p_ref[head, 0:seen, at] = probs
            ot_ref[rows, at] = dot(vt_s[rows, 0:seen], probs)

    o_s[...] = ot_ref[...].T.astype(BF16)
    start = pl.multiple_of(parity(meta_ref[0] & 3) * half, half)
    same_ref[...] = o_s[pl.ds(start, half), :]
    other_ref[...] = o_s[pl.ds(pl.multiple_of(half - start, half), half), :]


def attend_fast(meta, q, k, v):
    length, cols = q.shape
    pairs = cols // LANES
    block = pl.BlockSpec((length, LANES), lambda g, m: (0, g))
    half = pl.BlockSpec((length // 2, LANES), lambda g, m: (0, g))
    return call(
        attend_kernel,
        (pairs,),
        [block, block, block],
        [
            pl.BlockSpec((2, length, length), lambda g, m: (g, 0, 0)),
            pl.BlockSpec((LANES, length), lambda g, m: (g, 0)),
            half,
            half,
        ],
        [
            sds((2 * pairs, length, length), BF16),
            sds((cols, length), F32),
            sds((length // 2, cols), BF16),
            sds((length // 2, cols), BF16),
        ],
        (q, k, v),
        (meta,),
        scratch=[pltpu.VMEM((LANES, length), BF16), pltpu.VMEM((length, LANES), BF16)],
        est=cost(8 * length * length * cols, 4 * length * length * pairs + 10 * length * cols),
    )


def attend_back_kernel(
    meta_ref, q_ref, k_ref, v_ref, p_ref, ot_ref, go_ref, gx_ref, gy_ref, gd_ref,
    dq_ref, dk_ref, dv_ref, g_s, gt_s, kt_s, dqt_s, dk_s, dv_s,
):
    length = q_ref.shape[0]
    t = meta_ref[0] & 3
    for piece, who in ((go_ref, t), (gx_ref, t ^ 1), (gy_ref, t ^ 2), (gd_ref, t ^ 3)):
        start = pl.multiple_of(tok_block(who) * QUARTER, QUARTER)
        g_s[pl.ds(start, QUARTER), :] = piece[...]
    gt_s[...] = g_s[...].astype(F32).T
    kt_s[...] = k_ref[...].astype(F32).T.astype(BF16)
    dk_s[...] = jnp.zeros_like(dk_s)
    dv_s[...] = jnp.zeros_like(dv_s)
    scale = jnp.asarray(HEAD ** (-0.5), BF16)

    @pl.loop(0, 2)
    def _(head):
        rows = pl.ds(pl.multiple_of(head * HEAD, HEAD), HEAD)
        for j in range(length // QUARTER):
            at = slice(QUARTER * j, QUARTER * (j + 1))
            seen = QUARTER * (j + 1)
            query = head_lanes(q_ref[at, :], head) * scale
            grad = head_lanes(g_s[at, :], head)
            inner = jnp.sum(gt_s[rows, at] * ot_ref[rows, at], axis=0, keepdims=True)
            probs = p_ref[head, 0:seen, at]
            grad_probs = dot_nt(v_ref[0:seen, :], grad)
            grad_scores = (probs.astype(F32) * (grad_probs - inner)).astype(BF16)
            dv_s[0:seen, :] += dot(probs, grad)
            dk_s[0:seen, :] += dot(grad_scores, query)
            dqt_s[rows, at] = dot(kt_s[rows, 0:seen], grad_scores)

    dq_ref[...] = (dqt_s[...].T * (HEAD ** (-0.5))).astype(BF16)
    dk_ref[...] = dk_s[...].astype(BF16)
    dv_ref[...] = dv_s[...].astype(BF16)


def attend_back_fast(meta, q, k, v, probs, out_t, pieces):
    length, cols = q.shape
    pairs = cols // LANES
    block = pl.BlockSpec((length, LANES), lambda g, m: (0, g))
    piece = pl.BlockSpec((QUARTER, LANES), lambda g, m: (0, g))
    return call(
        attend_back_kernel,
        (pairs,),
        [
            block,
            block,
            block,
            pl.BlockSpec((2, length, length), lambda g, m: (g, 0, 0)),
            pl.BlockSpec((LANES, length), lambda g, m: (g, 0)),
            piece,
            piece,
            piece,
            piece,
        ],
        [block, block, block],
        [sds((length, cols), BF16)] * 3,
        (q, k, v, probs, out_t, *pieces),
        (meta,),
        scratch=[
            pltpu.VMEM((length, LANES), BF16),
            pltpu.VMEM((LANES, length), F32),
            pltpu.VMEM((LANES, length), BF16),
            pltpu.VMEM((LANES, length), F32),
            pltpu.VMEM((length, LANES), F32),
            pltpu.VMEM((length, LANES), F32),
        ],
        est=cost(16 * length * length * cols, 4 * length * length * pairs + 16 * length * cols),
    )


def mlp_kernel(enter, leave, has_own, n_pairs, *refs):
    refs = list(refs)
    meta_ref = refs.pop(0)

    def take(n):
        out = refs[:n]
        del refs[:n]
        return out

    if enter:
        groups_ref, counts_ref, x_ref, cot_ref, vec_ref, *head_refs, wof_ref = take(10)
    else:
        n2_in, low_in, gn_in, mlp_in = take(4)
    own_refs = take(1) if has_own else []
    pairs = [take(2) for _ in range(n_pairs)]
    if leave:
        outs = take(3 if enter else 2)
    else:
        outs = take(4)
    n2_s, low_s, h_s, gn_s, mlp_s, act_s, pre_s, buf, sem = refs
    blocks = own_refs[0].shape[0] if has_own else 0
    total = blocks + n_pairs
    depth = buf.shape[1]

    def fetch(i, slot):
        if has_own:
            @pl.when(i < blocks)
            def _():
                at = jnp.minimum(i, blocks - 1)
                pltpu.make_async_copy(own_refs[0].at[at], buf.at[slot], sem.at[slot]).start()

        for n, two in enumerate(pairs):
            @pl.when(i == blocks + n)
            def _(two=two):
                for m, ref in enumerate(two):
                    for part, rows in ((0, LANES), (LANES, LANES), (2 * LANES, BIAS_ROWS)):
                        pltpu.make_async_copy(
                            ref.at[pl.ds(part, rows)],
                            buf.at[slot, pl.ds(2 * part + m * rows, rows)],
                            sem.at[slot],
                        ).start()

    def settle(slot):
        pltpu.make_async_copy(buf.at[slot], buf.at[slot], sem.at[slot]).wait()

    fetch(0, 0)
    if enter:
        local = head_refs[0].shape[1]
        for n, ref in enumerate(head_refs):
            h_s[:, local * n : local * (n + 1)] = ref[...]
        resid = x_ref[0].astype(F32) + dot(h_s[...], wof_ref[...]) + vec_ref[4:5, :]
        if leave:
            outs[2][...] = resid
        xhat, _ = rows_stats(resid)
        n2_s[...] = (xhat * vec_ref[2:3, :] + vec_ref[3:4, :]).astype(BF16)
        weight = seq_weight_of(groups_ref, counts_ref)[:, 0:1]
        low_s[...] = (cot_ref[0].astype(F32) * weight).astype(BF16)
        gn_s[...] = jnp.zeros_like(gn_s)
        mlp_s[...] = jnp.zeros_like(mlp_s)
    else:
        n2_s[...] = n2_in[...]
        low_s[...] = low_in[...]
        gn_s[...] = gn_in[...]
        mlp_s[...] = mlp_in[...]

    def ahead(slot):
        tail = buf[slot, 2 * QUARTER : depth, 0:LANES].astype(F32)
        parts = [
            tail[n : n + 1, :] + tail[n + 1 : n + 2, :] + tail[n + 2 : n + 3, :]
            for n in range(0, depth - 2 * QUARTER, BIAS_ROWS)
        ]
        pre = dot_nt(n2_s[...], buf[slot, 0:QUARTER, :]) + jnp.concatenate(parts, axis=1)
        grad_act = dot_nt(low_s[...], buf[slot, QUARTER : 2 * QUARTER, :])
        root = math.sqrt(2.0 / math.pi)
        square = pre * pre
        turn = jnp.tanh(root * (pre + 0.044715 * (square * pre)))
        half = 0.5 * (1.0 + turn)
        slope = half + (0.5 * root) * pre * (1.0 - turn * turn) * (1.0 + 3.0 * 0.044715 * square)
        return (pre * half).astype(BF16), (grad_act * slope).astype(BF16)

    def behind(slot, act, grad_pre):
        gn_s[...] += dot(grad_pre, buf[slot, 0:QUARTER, :])
        mlp_s[...] += dot(act, buf[slot, QUARTER : 2 * QUARTER, :])

    settle(0)
    if total > 1:
        fetch(1, 1)
    act_s[0], pre_s[0] = ahead(0)

    @pl.loop(1, total)
    def _(i):
        slot = lax.rem(i, 3)
        settle(slot)

        @pl.when(i + 1 < total)
        def _():
            fetch(i + 1, lax.rem(i + 1, 3))

        old = (i + 1) & 1
        act, grad_pre = act_s[old], pre_s[old]
        new_act, new_pre = ahead(slot)
        behind(lax.rem(i + 2, 3), act, grad_pre)
        act_s[i & 1], pre_s[i & 1] = new_act, new_pre

    last = total - 1
    behind(last % 3, act_s[last & 1], pre_s[last & 1])
    if not leave:
        outs[2][...] = n2_s[...]
        outs[3][...] = low_s[...]
    outs[0][...] = gn_s[...].astype(outs[0].dtype)
    outs[1][...] = mlp_s[...].astype(outs[1].dtype)


def mlp_call(meta, flip, entry, state, own, pairs, leave):
    width = pairs[0][0].shape[1]
    enter = entry is not None
    rows = pl.BlockSpec((1, QUARTER, width), lambda i, m: (0, tok_block((m[0] & 3) ^ flip), 0))
    out = whole((QUARTER, width))
    any_ = pl.BlockSpec(memory_space=pl.ANY)
    local = width // 4
    if enter:
        groups, counts, x, cot, vec, heads, wof = entry
        head = pl.BlockSpec((QUARTER, local), lambda i, m: ((((m[0] & 3) ^ flip) >> 1) & 1, 0))
        specs = [smem(), smem(), rows, rows, whole(vec.shape)] + [head] * 4 + [whole(wof.shape)]
        args = [groups, counts, x, cot, vec, *heads, wof]
    else:
        specs = [out] * 4
        args = list(state)
    mine = [] if own is None else [own]
    flat = [ref for two in pairs for ref in two]
    if leave:
        kinds = [F32, F32, F32] if enter else [BF16, BF16]
    else:
        kinds = [F32, F32, BF16, BF16]
    depth = 2 * QUARTER + BIAS_ROWS * (QUARTER // LANES)
    hidden = QUARTER * ((0 if own is None else own.shape[0]) + len(pairs))
    return call(
        functools.partial(mlp_kernel, enter, leave, own is not None, len(pairs)),
        (1,),
        specs + [any_] * (len(mine) + len(flat)),
        [out] * len(kinds),
        [sds((QUARTER, width), kind) for kind in kinds],
        (*args, *mine, *flat),
        (meta,),
        scratch=[
            pltpu.VMEM((QUARTER, width), BF16),
            pltpu.VMEM((QUARTER, width), BF16),
            pltpu.VMEM((QUARTER, width), BF16),
            pltpu.VMEM((QUARTER, width), F32),
            pltpu.VMEM((QUARTER, width), F32),
            pltpu.VMEM((2, QUARTER, QUARTER), BF16),
            pltpu.VMEM((2, QUARTER, QUARTER), BF16),
            pltpu.VMEM((3, depth, width), BF16),
            pltpu.SemaphoreType.DMA((3,)),
        ],
        est=cost(
            8 * QUARTER * width * hidden + (2 * QUARTER * width * width if enter else 0),
            4 * width * hidden + 2 * width * width + 16 * QUARTER * width,
            QUARTER * hidden,
        ),
    )


def project_kernel(meta_ref, own_ref, *refs):
    wof_ref = refs[-1]
    core = (meta_ref[0] >> 2) & 1
    local = own_ref.shape[0]
    half = local // 2
    wof_ref[0:local, :] = own_ref[...]
    for n in range(3):
        for ref, at in ((refs[2 * n], core), (refs[2 * n + 1], 1 - core)):
            start = pl.multiple_of(local * (n + 1) + at * half, half)
            wof_ref[pl.ds(start, half), :] = ref[...]


def project(meta, own, packs, halves):
    local, width = own.shape
    half = local // 2
    skip = packs[0].shape[0] - half
    tail = pl.BlockSpec((pl.Element(half), pl.Element(width)), lambda i, m: (skip, 0))
    return call(
        project_kernel,
        (1,),
        [whole(own.shape)] + [tail] * 4 + [whole(h.shape) for h in halves],
        whole((4 * local, width)),
        sds((4 * local, width), BF16),
        (own, *packs, *halves),
        (meta,),
        est=cost(0, 16 * local * width),
    )


def resid_back_kernel(
    meta_ref, groups_ref, counts_ref, own_ref, recv_ref, resid_ref, cot_ref, vec_ref, wof_ref,
    gr_ref, o_ref, x_ref, y_ref, d_ref,
):
    weight = seq_weight_of(groups_ref, counts_ref)[:, 0:1]
    grad = own_ref[...] + recv_ref[...].astype(F32)
    xhat, rstd = rows_stats(resid_ref[...])
    total = cot_ref[0].astype(F32) * weight + norm_grad(xhat, rstd, vec_ref[2:3, :], grad)
    gr_ref[...] = total
    low = total.astype(BF16)
    local = wof_ref.shape[0] // 4
    for n, ref in enumerate((o_ref, x_ref, y_ref, d_ref)):
        ref[...] = dot_nt(low, wof_ref[local * n : local * (n + 1), :]).astype(BF16)


def resid_back(meta, groups, counts, own, recv, resid, cot, vec, wof):
    width = own.shape[1]
    local = wof.shape[0] // 4
    piece = whole((QUARTER, local))
    full = whole((QUARTER, width))
    return call(
        resid_back_kernel,
        (1,),
        [
            smem(),
            smem(),
            full,
            full,
            full,
            pl.BlockSpec((1, QUARTER, width), lambda i, m: (0, tok_block(m[0] & 3), 0)),
            whole(vec.shape),
            whole(wof.shape),
        ],
        [full, piece, piece, piece, piece],
        [sds((QUARTER, width), F32)] + [sds((QUARTER, local), BF16)] * 4,
        (groups, counts, own, recv, resid, cot, vec, wof),
        (meta,),
        est=cost(2 * QUARTER * width * width, 16 * QUARTER * width + 2 * width * width),
    )


def adapter_inner(dq, dv, up_s, cols):
    ups = up_s[...].astype(BF16)
    return ADAPTER_SCALE * (dot_nt(dq, ups[:, 0:cols]) + dot_nt(dv, ups[:, cols : 2 * cols]))


def fill_up(up_s, up_ref, cols):
    rank = up_ref.shape[1]
    up_s[...] = jnp.zeros_like(up_s)
    for copy in (0, 2):
        up_s[copy * rank : (copy + 1) * rank, 0:cols] = up_ref[0]
        up_s[(copy + 1) * rank : (copy + 2) * rank, cols : 2 * cols] = up_ref[1]


def split_inner(inner, rank):
    high = inner.astype(BF16)
    low = (inner - high.astype(F32)).astype(BF16)
    lane = lax.broadcasted_iota(jnp.int32, inner.shape, 1)
    return jnp.where(lane < 2 * rank, high.astype(F32), low.astype(F32))


def grads_kernel(
    meta_ref, groups_ref, counts_ref, dq_ref, dv_ref, up_ref, n_ref, lora_ref,
    grads_ref, up_s, dn_s, gu_s,
):
    i = pl.program_id(0)
    rank = up_ref.shape[1]
    cols = dq_ref.shape[1]

    @pl.when(i == 0)
    def _():
        fill_up(up_s, up_ref, cols)
        dn_s[...] = jnp.zeros_like(dn_s)
        gu_s[...] = jnp.zeros_like(gu_s)

    dq, dv = dq_ref[...], dv_ref[...]
    split = split_inner(adapter_inner(dq, dv, up_s, cols), rank)
    dn_s[...] += dot(split.T.astype(BF16), n_ref[...])
    lt = lora_ref[...].astype(F32).T.astype(BF16)
    gu_s[...] += ADAPTER_SCALE * dot(lt, jnp.concatenate([dq, dv], axis=1))

    @pl.when(i == pl.num_programs(0) - 1)
    def _():
        grads_ref[...] = jnp.zeros_like(grads_ref)
        grads_ref[0 : 2 * rank, :] = dn_s[0 : 2 * rank, :] + dn_s[2 * rank : 4 * rank, :]
        start = pl.multiple_of((meta_ref[0] & 3) * cols, cols)
        grads_ref[2 * rank : 3 * rank, pl.ds(start, cols)] = gu_s[0:rank, 0:cols]
        grads_ref[3 * rank : 4 * rank, pl.ds(start, cols)] = gu_s[rank : 2 * rank, cols : 2 * cols]
        weight = seq_weight_of(groups_ref, counts_ref)[:, 0:1]
        grads_ref[4 * rank : 4 * rank + 8, :] = jnp.broadcast_to(weight, (8, grads_ref.shape[1]))


def adapter_grads(meta, groups, counts, dq, dv, up, norm1, lora):
    length, cols = dq.shape
    width = norm1.shape[1]
    rank = up.shape[1]
    rows = 2 * QUARTER
    block = pl.BlockSpec((rows, cols), lambda i, m: (i, 0))
    lanes = pl.BlockSpec((rows, LANES), lambda i, m: (i, 0))
    return call(
        grads_kernel,
        (length // rows,),
        [
            smem(),
            smem(),
            block,
            block,
            pl.BlockSpec((2, rank, cols), lambda i, m: (0, 0, m[0] & 3)),
            pl.BlockSpec((rows, width), lambda i, m: (i, 0)),
            lanes,
        ],
        whole((4 * rank + 8, width)),
        sds((4 * rank + 8, width), F32),
        (groups, counts, dq, dv, up, norm1, lora),
        (meta,),
        scratch=[
            pltpu.VMEM((LANES, 2 * cols), F32),
            pltpu.VMEM((LANES, width), F32),
            pltpu.VMEM((LANES, 2 * cols), F32),
        ],
        est=cost(2 * length * width * LANES, 2 * length * width + 4 * length * cols),
    )


def input_back_kernel(
    meta_ref, dq_ref, dk_ref, dv_ref, w_ref, down_ref, up_ref,
    ox_ref, oy_ref, od_ref, own_ref, down_s, up_s,
):
    i = pl.program_id(0)
    rank = down_ref.shape[1]
    cols = dq_ref.shape[1]

    @pl.when(i == 0)
    def _():
        fill_up(up_s, up_ref, cols)
        down_s[...] = jnp.zeros_like(down_s)
        both = jnp.concatenate([down_ref[0], down_ref[1]], axis=0)
        down_s[0 : 2 * rank, :] = both
        down_s[2 * rank : 4 * rank, :] = both

    dq, dv = dq_ref[...], dv_ref[...]
    split = split_inner(adapter_inner(dq, dv, up_s, cols), rank)
    grad = (
        dot_nt(dq, w_ref[0])
        + dot_nt(dk_ref[...], w_ref[1])
        + dot_nt(dv, w_ref[2])
        + dot(split.astype(BF16), down_s[...].astype(BF16))
    )
    for n, ref in enumerate((ox_ref, oy_ref, od_ref, own_ref)):
        @pl.when(i == n)
        def _(ref=ref):
            ref[...] = grad.astype(ref.dtype)


def input_back(meta, dq, dk, dv, w, down_t, up):
    length, cols = dq.shape
    width = w.shape[1]
    rank = up.shape[1]

    def who(i, m):
        return tok_block((m[0] & 3) ^ jnp.where(i == 3, 0, i + 1))

    block = pl.BlockSpec((QUARTER, cols), lambda i, m: (who(i, m), 0))
    out = whole((QUARTER, width))
    return call(
        input_back_kernel,
        (4,),
        [
            block,
            block,
            block,
            whole(w.shape),
            whole(down_t.shape),
            pl.BlockSpec((2, rank, cols), lambda i, m: (0, 0, m[0] & 3)),
        ],
        [out, out, out, out],
        [sds((QUARTER, width), BF16)] * 3 + [sds((QUARTER, width), F32)],
        (dq, dk, dv, w, down_t, up),
        (meta,),
        scratch=[pltpu.VMEM((LANES, width), F32), pltpu.VMEM((LANES, 2 * cols), F32)],
        est=cost(6 * length * width * cols, 6 * width * cols + 6 * length * cols + 6 * length * width),
    )


def first_back_kernel(meta_ref, own_ref, a_ref, b_ref, c_ref, x_ref, gr_ref, vec_ref, out_ref):
    grad = own_ref[...] + a_ref[...].astype(F32) + b_ref[...].astype(F32) + c_ref[...].astype(F32)
    xhat, rstd = rows_stats(x_ref[0].astype(F32))
    out_ref[...] = (gr_ref[...] + norm_grad(xhat, rstd, vec_ref[0:1, :], grad)).astype(BF16)


def first_back(meta, own, pieces, x, grad_resid, vec):
    width = own.shape[1]
    full = whole((QUARTER, width))
    return call(
        first_back_kernel,
        (1,),
        [
            full,
            full,
            full,
            full,
            pl.BlockSpec((1, QUARTER, width), lambda i, m: (0, tok_block(m[0] & 3), 0)),
            full,
            whole(vec.shape),
        ],
        full,
        sds((QUARTER, width), BF16),
        (own, *pieces, x, grad_resid, vec),
        (meta,),
        est=cost(30 * QUARTER * width, 16 * QUARTER * width),
    )


def gather_kernel(scaled, first, meta_ref, *refs):
    refs = list(refs)
    if not first:
        refs.pop(0)
    if scaled:
        factor = scaled / refs.pop(0)[0:1, 0:1]
    out_ref = refs.pop()

    def put(start, ref):
        value = ref[...]
        if scaled:
            value = (value.astype(F32) * factor).astype(BF16)
        out_ref[0, start : start + ref.shape[0], :] = value

    if first:
        for n, ref in enumerate(refs):
            @pl.when(pl.program_id(0) == n)
            def _(ref=ref):
                put(0, ref)
    else:
        put(0, refs[0])
        put(refs[0].shape[0], refs[1])


def gather_rows(meta, pieces, scaled=0.0, total=None):
    width = pieces[0].shape[1]
    extra = [total] if scaled else []
    specs = [pl.BlockSpec((8, width), lambda i, m: (total.shape[0] // 8 - 1, 0))] if scaled else []
    result = sds((1, 4 * QUARTER, width), BF16)

    def out(base):
        return pl.BlockSpec(
            (1, QUARTER, width), lambda i, m: (0, tok_block((m[0] & 3) ^ (base + i)), 0)
        )

    part = call(
        functools.partial(gather_kernel, scaled, True),
        (3,),
        specs + [whole(p.shape) for p in pieces[:3]],
        out(0),
        result,
        (*extra, *pieces[:3]),
        (meta,),
        est=cost(0, 12 * QUARTER * width),
    )
    return call(
        functools.partial(gather_kernel, scaled, False),
        (1,),
        [pl.BlockSpec(memory_space=pl.ANY)] + specs + [whole(p.shape) for p in pieces[3:]],
        out(3),
        result,
        (part, *extra, *pieces[3:]),
        (meta,),
        est=cost(0, 4 * QUARTER * width),
        alias={1: 0},
    )


def update_kernel(tokens, devices, total_ref, d_ref, u_ref, md_ref, mu_ref, ad_ref, au_ref, *outs):
    gd_o, gu_o, md_o, mu_o, d_o, u_o, ad_o, au_o, cd_o, cu_o = outs
    rank = d_ref.shape[1]
    weight = total_ref[4 * rank : 4 * rank + 1, 0:1]
    mean_weight = weight / devices
    rate = RATE_BASE * math.sqrt(tokens)
    for c in range(2):
        for base, g_o, m_ref, m_o, w_ref, w_o, a_ref, a_o, c_o in (
            (0, gd_o, md_ref, md_o, d_ref, d_o, ad_ref, ad_o, cd_o),
            (2 * rank, gu_o, mu_ref, mu_o, u_ref, u_o, au_ref, au_o, cu_o),
        ):
            gradient = total_ref[base + c * rank : base + (c + 1) * rank, :] / (mean_weight * tokens)
            moment, new, average = update_step(gradient, m_ref[c], w_ref[c], a_ref[c], rate)
            g_o[c] = gradient
            m_o[c] = moment
            w_o[c] = new
            a_o[c] = average
            c_o[c] = new.astype(BF16)


def update(tokens, devices, total, down_t, up, mom_d, mom_u, avg_d, avg_u):
    shapes = [whole(total.shape)] + [whole(down_t.shape)] * 6
    kinds = [F32] * 8 + [BF16] * 2
    return call(
        functools.partial(update_kernel, float(tokens), float(devices)),
        (1,),
        shapes,
        [whole(down_t.shape)] * 10,
        [sds(down_t.shape, kind) for kind in kinds],
        (total, down_t, up, mom_d, mom_u, avg_d, avg_u),
        (),
        est=cost(0, 18 * 4 * down_t.size),
    )


def local_fast(
    dp_size,
    inputs,
    cotangent,
    groups,
    counts,
    vector_parameters,
    query_value_bias,
    hidden_bias,
    query_key_value_weight,
    attention_output_weight,
    hidden_weight,
    hidden_output_weight,
    adapter_down,
    adapter_up,
    momentum_down,
    momentum_up,
    average_down,
    average_up,
):
    axes = ("dp", "tensor")

    def send(value, dp_flip, t_flip):
        pairs = [
            (d * 4 + t, (d ^ dp_flip) * 4 + (t ^ t_flip)) for d in range(dp_size) for t in range(4)
        ]
        return lax.ppermute(value, axes, pairs)

    def plane(first, second, third):
        values = (first, second, third)
        return [send(value, 0, n + 1) for n, value in enumerate(values)]

    def swap(values):
        return [send(value, 1, 0) for value in values]

    half = QUARTER // 2

    def spread(own):
        from_x = send(own, 0, 1)
        from_y = send(own, 0, 2)
        cut_x, cut_y = from_x[:half], from_y[half:]
        return [own, from_x, from_y, send(cut_x, 0, 2), send(cut_y, 0, 1)]

    tensor_at = lax.axis_index("tensor")
    core = lax.axis_index("dp") & 1
    meta = (tensor_at + 4 * core).astype(jnp.int32).reshape(1)
    down_t = jnp.swapaxes(adapter_down, 1, 2)
    vec = vector_parameters
    length = inputs.shape[1]
    ffn = (hidden_weight, hidden_output_weight, hidden_bias)

    local_rows = attention_output_weight.shape[0] // 2
    mine = lax.dynamic_slice_in_dim(attention_output_weight, core * local_rows, local_rows, 0)
    xa, xb, ya, yb = fetch_packs(core.astype(jnp.int32).reshape(1), *ffn, attention_output_weight)
    got_d = send(mine, 0, 3)
    got_x, got_y = send(xa, 0, 1), send(ya, 0, 2)

    q, k, v, norm1, lora = qkv(
        meta, inputs, vec, query_key_value_weight, query_value_bias, down_t, adapter_up
    )
    probs, out_t, same, other = attend_fast(meta, q, k, v)
    heads = [same] + plane(other, other, same)
    late_x, late_y = send(xb, 0, 1), send(yb, 0, 2)
    swap_x, swap_y, swap_d = swap((got_x, got_y, got_d))
    own = pack(*ffn)
    wof = project(
        meta, attention_output_weight, (got_x, swap_x, got_y, swap_y), (got_d, swap_d)
    )
    entry = (groups, counts, inputs, cotangent, vec, heads, wof)
    early = [(got_x, got_y), (swap_x, swap_y)]
    gn, mlp, n2, low = mlp_call(meta, 3, entry, None, own, early, False)
    late = [(late_x, late_y), tuple(swap((late_x, late_y)))]
    gn_pair, mlp_pair = mlp_call(meta, 3, None, (n2, low, gn, mlp), None, late, True)
    gn_recv = send(gn_pair, 0, 3)
    mlp_recv = send(mlp_pair, 0, 3)
    gn_own, mlp_own, resid = mlp_call(meta, 0, entry, None, own, early + late, True)
    grad_resid, g_own, g_x, g_y, g_d = resid_back(
        meta, groups, counts, gn_own, gn_recv, resid, cotangent, vec, wof
    )
    pieces = [g_own] + plane(g_x, g_y, g_d)
    out_own = (resid + mlp_own + mlp_recv.astype(F32) + vec[5]).astype(BF16)
    out_all = spread(out_own)

    dq, dk, dv = attend_back_fast(meta, q, k, v, probs, out_t, pieces)
    gx, gy, gd, g1_own = input_back(
        meta, dq, dk, dv, query_key_value_weight, down_t, adapter_up
    )
    g1 = plane(gx, gy, gd)
    total = adapter_grads(meta, groups, counts, dq, dv, adapter_up, norm1, lora)
    sum_x, sum_y, sum_d = plane(total, total, total)
    total = (total + sum_x) + (sum_y + sum_d)
    step = 1
    while step < dp_size:
        total = total + send(total, step, 0)
        step *= 2
    in_own = first_back(meta, g1_own, g1, inputs, grad_resid, vec)
    in_all = spread(in_own)
    block_out = gather_rows(meta, out_all)
    copies = dp_size * 4
    input_grad = gather_rows(meta, in_all, scaled=float(copies), total=total)
    results = update(
        dp_size * length,
        copies,
        total,
        down_t,
        adapter_up,
        jnp.swapaxes(momentum_down, 1, 2),
        momentum_up,
        jnp.swapaxes(average_down, 1, 2),
        average_up,
    )
    results = [
        jnp.swapaxes(value, 1, 2) if number % 2 == 0 else value
        for number, value in enumerate(results)
    ]
    return (block_out, input_grad, *results)


def solution(mesh):
    in_specs = (
        P("dp", None, None),
        P("dp", None, None),
        P("dp"),
        P(),
        P(),
        P(None, "tensor"),
        P("tensor"),
        P(None, None, "tensor"),
        P("tensor", None),
        P(None, "tensor"),
        P("tensor", None),
        P(),
        P(),
        P(),
        P(),
        P(),
        P(),
    )
    out_specs = (
        P("dp", None, None),
        P("dp", None, None),
        P(),
        P(),
        P(),
        P(),
        P(),
        P(),
        P(),
        P(),
        P(),
        P(),
    )
    dp_size = mesh.shape["dp"]
    small = mesh.shape["tensor"] == 4 and dp_size & (dp_size - 1) == 0 and dp_size > 1

    def body(*args):
        if small and args[0].shape[0] == 1 and args[0].shape[1] == 4 * QUARTER:
            return local_fast(dp_size, *args)
        return local(*args)

    return jax.shard_map(body, mesh=mesh, in_specs=in_specs, out_specs=out_specs, check_vma=False)
```
